32 devices in a mesh: section: 4 (over y, x), rep: 8 (over z, core).
Axes of the slice: x: 2, y: 2, z: 4, core: 2. Of those that a mesh axis runs over, the one named last changes fastest.
Arguments:
- x_in: bfloat16 [1024, 4096], P('rep'), may hold values from -6 to 6
- cot: bfloat16 [1024, 4096], P('rep'), may hold values from -6 to 6
- w_q: bfloat16 [4, 4096, 128], P('section', 'rep'), may hold values from -0.09375 to 0.09375
- w_k: bfloat16 [4, 4096, 128], P('section', 'rep'), may hold values from -0.09375 to 0.09375
- w_v: bfloat16 [4, 4096, 128], P('section', 'rep'), may hold values from -0.09375 to 0.09375
- w_out: bfloat16 [4, 4096, 128], P('section', 'rep'), may hold values from -0.5 to 0.5
- gains: float32 [4, 4096], P('section'), may hold values from 0.5 to 1.5
- offsets: int32 [4, 8], replicated, may hold values from 0 to 7
- counts: int32 [4, 8], replicated, may hold values from 1 to 8
Outputs:
- grad_q: float32 [4, 4096, 128], P('section', 'rep')
- grad_k: float32 [4, 4096, 128], P('section', 'rep')
- grad_v: float32 [4, 4096, 128], P('section', 'rep')
- grad_o: float32 [4, 4096, 128], P('section', 'rep')
The draws below stay inside these ranges and needn't reach their ends.
All inputs are finite; a program needn't handle non-finite values.
Results may differ from the reference program's by a relative error of at most 0.023.
Values may be sent and summed in bfloat16 or wider, within the bound.
A program may use at most 64 MiB of HBM per device.

```python
import jax
import jax.numpy as jnp
from jax import lax

D = 4096
HD = 128
MB = 8
ROWS = 16
TOKENS = 1024
N_SECTION = 4
N_REP = 8


def touch_ends(array, key, smallest, top_value):
    shape = array.shape
    index_at = [jax.random.randint(jax.random.fold_in(key, axis), (), 0, shape[axis]) for axis in range(len(shape))]
    array = array.at[tuple(index_at)].set(smallest)
    longest = shape.index(max(shape))
    index_at[longest] = (index_at[longest] + 1) % shape[longest]
    return array.at[tuple(index_at)].set(top_value)


def block_levels(stream_key, shape, shards, low, largest):
    factor_of = 1.0
    for axis_at, shards_of in shards:
        heights = jax.random.uniform(jax.random.fold_in(jax.random.fold_in(stream_key, 6), axis_at), (shards_of,), jnp.float32, low / len(shards), largest / len(shards))
        factor_of = factor_of * jnp.repeat(jnp.exp(heights), shape[axis_at] // shards_of).reshape((-1,) + (1,) * (len(shape) - 1 - axis_at))
    return factor_of


def gaussian(own_key, shape, spread, limit, cuts=(), kind=jnp.bfloat16):
    level = block_levels(own_key, shape, cuts, -0.22, 0.18) if cuts else 1.0
    drawn = jax.random.normal(own_key, shape, jnp.float32) * spread * level
    return jnp.minimum(jnp.maximum(drawn, -limit), limit).astype(kind)


def setup_inputs(seed: int = 0) -> dict:
    streams_of = jax.random.split(jax.random.key(seed), 10)
    return {
        "x_in": gaussian(streams_of[0], (TOKENS, D), 1.0, 6.0, ((0, 8),)),
        "cot": gaussian(streams_of[1], (TOKENS, D), 1.0, 6.0, ((0, 8),)),
        "w_q": gaussian(streams_of[2], (N_SECTION, D, HD), D ** -0.5, 0.09375, ((0, 4), (1, 8))),
        "w_k": gaussian(streams_of[3], (N_SECTION, D, HD), D ** -0.5, 0.09375, ((0, 4), (1, 8))),
        "w_v": gaussian(streams_of[4], (N_SECTION, D, HD), D ** -0.5, 0.09375, ((0, 4), (1, 8))),
        "w_out": gaussian(streams_of[5], (N_SECTION, D, HD), HD ** -0.5, 0.5, ((0, 4), (1, 8))),
        "gains": jnp.clip(1.0 + 0.1 * jax.random.normal(streams_of[6], (N_SECTION, D), jnp.float32), 0.5, 1.5),
        "offsets": touch_ends(jax.random.randint(streams_of[7], (N_SECTION, MB), 0, N_REP), jax.random.fold_in(streams_of[7], 1), 0, N_REP - 1).astype(jnp.int32),
        "counts": touch_ends(jax.random.randint(streams_of[8], (N_SECTION, N_REP), 1, MB + 1), jax.random.fold_in(streams_of[8], 1), 1, MB).astype(jnp.int32),
    }


EPSILON = 1e-05

def attend(query, key, scale):
    scores = jnp.einsum('gid,gjd->gij', query.astype(jnp.float32), key.astype(jnp.float32)) * scale
    causal = jnp.arange(ROWS)[:, None] >= jnp.arange(ROWS)[None, :]
    expo = jnp.exp(jnp.where(causal[None], scores, -1e+30))
    return expo / lax.optimization_barrier(jnp.sum(expo, axis=-1, keepdims=True))

def replica_sum(left, right):
    width_left = left.shape[-1]
    width_right = right.shape[-1]
    left_blocks = left.reshape(N_REP, MB * ROWS, width_left).astype(jnp.float32)
    right_blocks = right.reshape(N_REP, MB * ROWS, width_right).astype(jnp.float32)
    partial_grads = jnp.einsum('rtd,rth->rdh', left_blocks, right_blocks).astype(jnp.bfloat16)
    partial_grads = lax.optimization_barrier(partial_grads)
    return lax.optimization_barrier(jnp.sum(partial_grads.astype(jnp.float32), axis=0))

def reference(x_in, cot, w_q, w_k, w_v, w_out, gains, offsets, counts):
    scale = HD ** (-0.5)
    groups = N_REP * MB
    rep_ids = jnp.arange(N_REP, dtype=jnp.int32)
    batch_ids = jnp.arange(MB, dtype=jnp.int32)
    landing_sum = jnp.cumsum(offsets, axis=0) % N_REP
    current = x_in
    saved = []
    for section_no in range(N_SECTION):
        landing = (rep_ids[:, None] + landing_sum[section_no][None, :]) % N_REP
        allowed = counts[section_no][landing]
        keep_flat = (batch_ids[None, :] < allowed).astype(jnp.float32).reshape(-1)
        keep_rows = jnp.repeat(keep_flat, ROWS)[:, None]
        x_float = current.astype(jnp.float32)
        rinv = lax.rsqrt(lax.optimization_barrier(jnp.mean(x_float * x_float, axis=-1, keepdims=True)) + EPSILON)
        normed = (x_float * rinv * gains[section_no]).astype(jnp.bfloat16)
        query = jnp.dot(normed, w_q[section_no], preferred_element_type=jnp.float32).astype(jnp.bfloat16).reshape(groups, ROWS, HD)
        key = jnp.dot(normed, w_k[section_no], preferred_element_type=jnp.float32).astype(jnp.bfloat16).reshape(groups, ROWS, HD)
        value = jnp.dot(normed, w_v[section_no], preferred_element_type=jnp.float32).astype(jnp.bfloat16).reshape(groups, ROWS, HD)
        probs_low = attend(query, key, scale).astype(jnp.bfloat16)
        heads = jnp.einsum('gij,gjd->gid', probs_low.astype(jnp.float32), value.astype(jnp.float32)).astype(jnp.bfloat16).reshape(-1, HD)
        output = jnp.dot(heads, w_out[section_no].T, preferred_element_type=jnp.float32)
        saved.append((current, normed, query, key, value, heads, keep_rows))
        current = (x_float + keep_rows * output).astype(jnp.bfloat16)
    back = cot
    list_q, list_k, list_v, list_o = ([], [], [], [])
    for section_no in range(N_SECTION - 1, -1, -1):
        layer_in, normed, query, key, value, heads, keep_rows = saved[section_no]
        grad_float = back.astype(jnp.float32)
        grad_rows = (keep_rows * grad_float).astype(jnp.bfloat16)
        d_heads = jnp.dot(grad_rows, w_out[section_no], preferred_element_type=jnp.float32).astype(jnp.bfloat16).reshape(groups, ROWS, HD)
        probs = attend(query, key, scale)
        probs_low = probs.astype(jnp.bfloat16)
        d_value = jnp.einsum('gij,gid->gjd', probs_low.astype(jnp.float32), d_heads.astype(jnp.float32)).astype(jnp.bfloat16)
        d_probs = jnp.einsum('gid,gjd->gij', d_heads.astype(jnp.float32), value.astype(jnp.float32))
        d_score = (probs * (d_probs - lax.optimization_barrier(jnp.sum(probs * d_probs, axis=-1, keepdims=True))) * scale).astype(jnp.bfloat16)
        d_query = jnp.einsum('gij,gjd->gid', d_score.astype(jnp.float32), key.astype(jnp.float32)).astype(jnp.bfloat16).reshape(-1, HD)
        d_key = jnp.einsum('gij,gid->gjd', d_score.astype(jnp.float32), query.astype(jnp.float32)).astype(jnp.bfloat16).reshape(-1, HD)
        d_value = d_value.reshape(-1, HD)
        d_normed = jnp.dot(d_query, w_q[section_no].T, preferred_element_type=jnp.float32)
        d_normed = d_normed + jnp.dot(d_key, w_k[section_no].T, preferred_element_type=jnp.float32)
        d_normed = d_normed + jnp.dot(d_value, w_v[section_no].T, preferred_element_type=jnp.float32)
        list_q.append(replica_sum(normed, d_query))
        list_k.append(replica_sum(normed, d_key))
        list_v.append(replica_sum(normed, d_value))
        list_o.append(replica_sum(grad_rows, heads))
        x_float = layer_in.astype(jnp.float32)
        rinv = lax.rsqrt(lax.optimization_barrier(jnp.mean(x_float * x_float, axis=-1, keepdims=True)) + EPSILON)
        scaled = d_normed * gains[section_no]
        d_input = rinv * (scaled - x_float * rinv * rinv * lax.optimization_barrier(jnp.mean(scaled * x_float, axis=-1, keepdims=True)))
        back = (grad_float + d_input).astype(jnp.bfloat16)
    grad_q = jnp.stack(list_q[::-1])
    grad_k = jnp.stack(list_k[::-1])
    grad_v = jnp.stack(list_v[::-1])
    grad_o = jnp.stack(list_o[::-1])
    return (grad_q, grad_k, grad_v, grad_o)
```

```python
import functools

import jax
import jax.numpy as jnp
from jax import lax
from jax.experimental import pallas as pl
from jax.experimental.pallas import tpu as pltpu
from jax.sharding import PartitionSpec as P


MB = 8
ROWS = 16


EPSILON = 1e-05


def from_behind(block, axis, distance):
    devices = range(lax.axis_size(axis))
    route = [(i - distance, i) for i in devices if i - distance in devices]
    return lax.ppermute(block, axis, route)


def attend(query, key, scale):
    rows_here = query.shape[0]
    scores = jnp.einsum("id,jd->ij", query, key, preferred_element_type=jnp.float32) * scale
    causal = jnp.arange(rows_here)[:, None] >= jnp.arange(rows_here)[None, :]
    expo = jnp.exp(jnp.where(causal, scores, -1e30))
    return expo / jnp.sum(expo, axis=-1, keepdims=True)


def forward_layer(layer_in, gain, weights, keep):
    weight_q, weight_k, weight_v, weight_o = weights
    scale = weight_q.shape[1] ** (-0.5)
    x_float = layer_in.astype(jnp.float32)
    rinv = lax.rsqrt(jnp.mean(x_float * x_float, axis=-1, keepdims=True) + EPSILON)
    normed = (x_float * rinv * gain).astype(jnp.bfloat16)
    query = jnp.dot(normed, weight_q, preferred_element_type=jnp.float32).astype(jnp.bfloat16)
    key = jnp.dot(normed, weight_k, preferred_element_type=jnp.float32).astype(jnp.bfloat16)
    value = jnp.dot(normed, weight_v, preferred_element_type=jnp.float32).astype(jnp.bfloat16)
    probs_low = attend(query, key, scale).astype(jnp.bfloat16)
    heads = jnp.dot(probs_low, value, preferred_element_type=jnp.float32).astype(jnp.bfloat16)
    output = lax.dot_general(
        heads, weight_o, (((1,), (1,)), ((), ())), preferred_element_type=jnp.float32
    )
    result = (x_float + keep * output).astype(jnp.bfloat16)
    return (result, normed, query, key, value, heads)


def backward_layer(grad_in, layer_in, query, key, value, gain, weights, keep):
    weight_q, weight_k, weight_v, weight_o = weights
    scale = weight_q.shape[1] ** (-0.5)
    grad_float = grad_in.astype(jnp.float32)
    grad_rows = (keep * grad_float).astype(jnp.bfloat16)
    d_heads = jnp.dot(grad_rows, weight_o, preferred_element_type=jnp.float32).astype(jnp.bfloat16)
    probs = attend(query, key, scale)
    probs_low = probs.astype(jnp.bfloat16)
    d_value = jnp.einsum(
        "ij,id->jd", probs_low, d_heads, preferred_element_type=jnp.float32
    ).astype(jnp.bfloat16)
    d_probs = jnp.einsum("id,jd->ij", d_heads, value, preferred_element_type=jnp.float32)
    d_score = (probs * (d_probs - jnp.sum(probs * d_probs, axis=-1, keepdims=True)) * scale).astype(
        jnp.bfloat16
    )
    d_query = jnp.dot(d_score, key, preferred_element_type=jnp.float32).astype(jnp.bfloat16)
    d_key = jnp.einsum("ij,id->jd", d_score, query, preferred_element_type=jnp.float32).astype(
        jnp.bfloat16
    )
    contract = (((1,), (1,)), ((), ()))
    d_normed = lax.dot_general(d_query, weight_q, contract, preferred_element_type=jnp.float32)
    d_normed = d_normed + lax.dot_general(
        d_key, weight_k, contract, preferred_element_type=jnp.float32
    )
    d_normed = d_normed + lax.dot_general(
        d_value, weight_v, contract, preferred_element_type=jnp.float32
    )
    x_float = layer_in.astype(jnp.float32)
    rinv = lax.rsqrt(jnp.mean(x_float * x_float, axis=-1, keepdims=True) + EPSILON)
    scaled = d_normed * gain
    d_input = rinv * (
        scaled - x_float * rinv * rinv * jnp.mean(scaled * x_float, axis=-1, keepdims=True)
    )
    return ((grad_float + d_input).astype(jnp.bfloat16), grad_rows, d_query, d_key, d_value)


def store_slot(store, value, slot_at, is_valid):
    old_value = lax.dynamic_index_in_dim(store, slot_at, 0, keepdims=False)
    fresh = jnp.where(is_valid, value, old_value)
    return lax.dynamic_update_index_in_dim(store, fresh, slot_at, 0)


def zeros_like_all(values):
    return tuple((jnp.zeros(value.shape, value.dtype) for value in values))


def pick_slot(store, slot_at):
    return lax.dynamic_index_in_dim(store, slot_at, 0, keepdims=False)


def local_grad(left, right):
    width_left = left.shape[-1]
    width_right = right.shape[-1]
    return jnp.einsum(
        "td,th->dh",
        left.reshape(-1, width_left),
        right.reshape(-1, width_right),
        preferred_element_type=jnp.float32,
    )


def pipelined(x_in, cot, w_q, w_k, w_v, w_out, gains, offsets, counts):
    section_count = lax.axis_size("section")
    rep_count = lax.axis_size("rep")
    section_pos = lax.axis_index("section")
    rep_pos = lax.axis_index("rep")
    weights = (
        lax.all_gather(w_q[0], "rep", axis=0, tiled=True),
        lax.all_gather(w_k[0], "rep", axis=0, tiled=True),
        lax.all_gather(w_v[0], "rep", axis=0, tiled=True),
        lax.all_gather(w_out[0], "rep", axis=0, tiled=True),
    )
    width = weights[0].shape[0]
    head_size = weights[0].shape[1]
    gain = gains[0]
    landing_sum = jnp.cumsum(offsets, axis=0) % rep_count
    my_offsets = lax.dynamic_index_in_dim(landing_sum, section_pos, 0, keepdims=False)
    landing = (rep_pos + my_offsets) % rep_count
    count_row = lax.dynamic_index_in_dim(counts, section_pos, 0, keepdims=False)
    match_rep = landing[:, None] == jnp.arange(rep_count, dtype=jnp.int32)[None, :]
    allowed = jnp.sum(jnp.where(match_rep, count_row[None, :], 0), axis=1)
    keeps = (jnp.arange(MB, dtype=jnp.int32) < allowed).astype(jnp.float32)
    inputs = x_in.reshape(MB, ROWS, width)
    top_grads = cot.reshape(MB, ROWS, width)
    tick_count = section_count + MB - 1
    row_block = jnp.zeros((ROWS, width), jnp.bfloat16)
    head_block = jnp.zeros((ROWS, head_size), jnp.bfloat16)

    def forward_tick(tick_no, carry):
        inbox, saved_in, saved_normed, saved_q, saved_k, saved_v, saved_heads = carry
        batch_pos = tick_no - section_pos
        is_valid = (batch_pos >= 0) & (batch_pos < MB)
        batch_at = jnp.clip(batch_pos, 0, MB - 1)
        own_rows = pick_slot(inputs, batch_at)
        layer_in = jnp.where(section_pos == 0, own_rows, inbox)
        keep = pick_slot(keeps, batch_at)
        blank = (row_block, row_block, head_block, head_block, head_block, head_block)
        made = lax.cond(
            is_valid,
            lambda rows_in: forward_layer(rows_in, gain, weights, keep),
            lambda rows_in: zeros_like_all(blank),
            layer_in,
        )
        result, normed, query, key, value, heads = made
        saved_in = store_slot(saved_in, layer_in, batch_at, is_valid)
        saved_normed = store_slot(saved_normed, normed, batch_at, is_valid)
        saved_q = store_slot(saved_q, query, batch_at, is_valid)
        saved_k = store_slot(saved_k, key, batch_at, is_valid)
        saved_v = store_slot(saved_v, value, batch_at, is_valid)
        saved_heads = store_slot(saved_heads, heads, batch_at, is_valid)
        inbox = from_behind(result, "section", 1)
        return (inbox, saved_in, saved_normed, saved_q, saved_k, saved_v, saved_heads)

    wide_store = jnp.zeros((MB, ROWS, width), jnp.bfloat16)
    head_store = jnp.zeros((MB, ROWS, head_size), jnp.bfloat16)
    start_fwd = (row_block, wide_store, wide_store, head_store, head_store, head_store, head_store)
    _, saved_in, saved_normed, saved_q, saved_k, saved_v, saved_heads = lax.fori_loop(
        0, tick_count, forward_tick, start_fwd
    )

    def backward_tick(tick_no, carry):
        inbox, saved_rows, saved_dq, saved_dk, saved_dv = carry
        batch_pos = tick_no - (section_count - 1 - section_pos)
        is_valid = (batch_pos >= 0) & (batch_pos < MB)
        batch_at = jnp.clip(batch_pos, 0, MB - 1)
        grad_in = jnp.where(section_pos == section_count - 1, pick_slot(top_grads, batch_at), inbox)
        layer_in = pick_slot(saved_in, batch_at)
        query = pick_slot(saved_q, batch_at)
        key = pick_slot(saved_k, batch_at)
        value = pick_slot(saved_v, batch_at)
        keep = pick_slot(keeps, batch_at)
        blank = (row_block, row_block, head_block, head_block, head_block)
        made = lax.cond(
            is_valid,
            lambda rows_in: backward_layer(
                rows_in, layer_in, query, key, value, gain, weights, keep
            ),
            lambda rows_in: zeros_like_all(blank),
            grad_in,
        )
        grad_back, grad_rows, d_query, d_key, d_value = made
        saved_rows = store_slot(saved_rows, grad_rows, batch_at, is_valid)
        saved_dq = store_slot(saved_dq, d_query, batch_at, is_valid)
        saved_dk = store_slot(saved_dk, d_key, batch_at, is_valid)
        saved_dv = store_slot(saved_dv, d_value, batch_at, is_valid)
        inbox = from_behind(grad_back, "section", -1)
        return (inbox, saved_rows, saved_dq, saved_dk, saved_dv)

    start_bwd = (row_block, wide_store, head_store, head_store, head_store)
    _, saved_rows, saved_dq, saved_dk, saved_dv = lax.fori_loop(
        0, tick_count, backward_tick, start_bwd
    )
    full_q = local_grad(saved_normed, saved_dq)
    full_k = local_grad(saved_normed, saved_dk)
    full_v = local_grad(saved_normed, saved_dv)
    full_o = local_grad(saved_rows, saved_heads)
    share_width = width // rep_count
    totals = (
        lax.psum(full_q.astype(jnp.bfloat16), "rep").astype(jnp.float32),
        lax.psum(full_k.astype(jnp.bfloat16), "rep").astype(jnp.float32),
        lax.psum(full_v.astype(jnp.bfloat16), "rep").astype(jnp.float32),
        lax.psum(full_o.astype(jnp.bfloat16), "rep").astype(jnp.float32),
    )
    parts = tuple(
        (lax.dynamic_slice_in_dim(total, rep_pos * share_width, share_width, 0) for total in totals)
    )
    return (parts[0][None], parts[1][None], parts[2][None], parts[3][None])


F32 = jnp.float32
BF16 = jnp.bfloat16
VMEM_LIMIT = 60 * 1024 * 1024


def vmem_specs(count):
    return [pl.BlockSpec(memory_space=pltpu.VMEM)] * count


def exchange_kernel(plan, axes, *refs):
    count = len(plan)
    ins, outs = refs[:count], refs[count : 2 * count]
    sems = refs[2 * count :]
    barrier = pltpu.get_barrier_semaphore()
    waits = 0
    for axis, size in axes:
        me = lax.axis_index(axis)
        for step in range(1, size):
            peer = lax.rem(me + step, size)
            pl.semaphore_signal(
                barrier, inc=1, device_id={axis: peer}, device_id_type=pl.DeviceIdType.MESH
            )
            waits += 1
    pl.semaphore_wait(barrier, waits)
    copies = []
    for i, (axis, size, split) in enumerate(plan):
        send, recv = sems[2 * i], sems[2 * i + 1]
        me = lax.axis_index(axis)
        for step in range(1, size):
            peer = lax.rem(me + step, size)
            copy = pltpu.make_async_remote_copy(
                src_ref=ins[i].at[peer] if split else ins[i],
                dst_ref=outs[i].at[me],
                send_sem=send.at[step],
                recv_sem=recv.at[step],
                device_id={axis: peer},
                device_id_type=pl.DeviceIdType.MESH,
            )
            copy.start()
            copies.append((i, axis, size, split, step, copy))
    for i, (axis, size, split) in enumerate(plan):
        me = lax.axis_index(axis)
        own = ins[i].at[me] if split else ins[i]
        outs[i][me] = own[...]
    for i, axis, size, split, step, copy in copies:
        copy.wait_send()
        me = lax.axis_index(axis)
        source = lax.rem(me + size - step, size)
        pltpu.make_async_remote_copy(
            src_ref=outs[i].at[source],
            dst_ref=outs[i].at[source],
            send_sem=sems[2 * i].at[step],
            recv_sem=sems[2 * i + 1].at[step],
            device_id={axis: source},
            device_id_type=pl.DeviceIdType.MESH,
        ).wait_recv()


def exchange(items, collective_id):
    plan, shapes, scratch, names = [], [], [], []
    for array, axis, split in items:
        size = lax.axis_size(axis)
        plan.append((axis, size, split))
        block = array.shape[1:] if split else array.shape
        shapes.append(jax.ShapeDtypeStruct((size,) + block, array.dtype))
        scratch += [pltpu.SemaphoreType.DMA((size,)), pltpu.SemaphoreType.DMA((size,))]
        if (axis, size) not in names:
            names.append((axis, size))
    return pl.pallas_call(
        functools.partial(exchange_kernel, tuple(plan), tuple(names)),
        out_shape=shapes,
        in_specs=vmem_specs(len(items)),
        out_specs=vmem_specs(len(items)),
        scratch_shapes=scratch,
        compiler_params=pltpu.CompilerParams(
            collective_id=collective_id, has_side_effects=True, vmem_limit_bytes=VMEM_LIMIT
        ),
    )(*[array for array, _, _ in items])


def dot(left, right, dims=((1,), (0,))):
    return lax.dot_general(left, right, (dims, ((), ())), preferred_element_type=F32)


def project_kernel(x_ref, c_ref, wt_ref, w_ref, g_ref, zx_ref, zc_ref):
    reps, rows, shard = x_ref.shape
    sections = w_ref.shape[0]
    head = wt_ref.shape[0]
    x_all = x_ref[...].reshape(reps * rows, shard)
    c_all = c_ref[...].reshape(reps * rows, shard)
    both = jnp.concatenate([x_all, wt_ref[...]], axis=0)
    wide = both.astype(F32)

    def put(block, at):
        block = block.astype(BF16)
        width = block.shape[1]
        zx_ref[:, 0:rows, at : at + width] = block[0 : reps * rows].reshape(reps, rows, width)
        zx_ref[:, rows:, at : at + width] = block[reps * rows :].reshape(reps, head // reps, width)

    for s in range(sections):
        at = s * 4 * head
        scaled = (wide * g_ref[s]).astype(BF16)
        put(dot(scaled, w_ref[s, :, 0 : 3 * head]), at)
        w_o = w_ref[s, :, 3 * head :]
        put(dot(both, w_o), at + 3 * head)
        zc_ref[:, :, s * head : (s + 1) * head] = dot(c_all, w_o).astype(BF16).reshape(
            reps, rows, head
        )


def chain_kernel(scale, x_ref, zx_ref, zc_ref, m_ref, keep_ref, out_ref, scal_ref):
    sections = m_ref.shape[0]
    head = m_ref.shape[1]
    rows, width = x_ref.shape
    wide = 4 * head
    x_float = x_ref[...].astype(F32)
    square = jnp.sum(x_float * x_float, axis=1, keepdims=True)
    z = jnp.sum(zx_ref[:, 0:rows, :].astype(F32), axis=0)
    back = jnp.sum(zc_ref[...].astype(F32), axis=0)
    row = lax.broadcasted_iota(jnp.int32, (rows, rows), 0)
    col = lax.broadcasted_iota(jnp.int32, (rows, rows), 1)
    allowed = (row >= col) & (row // ROWS == col // ROWS)
    y = [z[:, s * wide : s * wide + 3 * head] for s in range(sections)]
    acto = [z[:, s * wide + 3 * head : (s + 1) * wide] for s in range(sections)]
    saved = []
    for s in range(sections):
        keep = keep_ref[:, s : s + 1]
        rinv = lax.rsqrt(jnp.maximum(square, 0.0) / width + EPSILON)
        qkv = (y[s] * rinv).astype(BF16)
        query, key, value = qkv[:, 0:head], qkv[:, head : 2 * head], qkv[:, 2 * head :]
        scores = dot(query, key, ((1,), (1,))) * scale
        expo = jnp.exp(jnp.where(allowed, scores, -1e30))
        probs = expo / jnp.sum(expo, axis=1, keepdims=True)
        low = probs.astype(BF16)
        heads = dot(low, value).astype(BF16)
        kept = heads.astype(F32) * keep
        kept_low = kept.astype(BF16)
        saved.append((rinv, query, key, value, probs, low, acto[:], y[s]))
        out_ref[:, s * wide + 3 * head : (s + 1) * wide] = heads
        moved = dot(kept_low, m_ref[s])
        square = square + jnp.sum(
            kept * (2.0 * acto[s] + moved[:, s * wide + 3 * head : (s + 1) * wide]),
            axis=1,
            keepdims=True,
        )
        for t in range(sections):
            if t > s:
                y[t] = y[t] + moved[:, t * wide : t * wide + 3 * head]
            acto[t] = acto[t] + moved[:, t * wide + 3 * head : (t + 1) * wide]
    bo = [back[:, s * head : (s + 1) * head] for s in range(sections)]
    lane = lax.broadcasted_iota(jnp.int32, (rows, head), 1)
    scal = jnp.zeros((rows, head), F32)
    for s in range(sections - 1, -1, -1):
        keep = keep_ref[:, s : s + 1]
        rinv, query, key, value, probs, low, act_o, y_s = saved[s]
        d_heads = (keep * bo[s]).astype(BF16)
        d_value = dot(low, d_heads, ((0,), (0,))).astype(BF16)
        d_probs = dot(d_heads, value, ((1,), (1,)))
        d_score = (
            probs * (d_probs - jnp.sum(probs * d_probs, axis=1, keepdims=True)) * scale
        ).astype(BF16)
        d_query = dot(d_score, key).astype(BF16)
        d_key = dot(d_score, query, ((0,), (0,))).astype(BF16)
        grads = jnp.concatenate([d_query, d_key, d_value], axis=1)
        out_ref[:, s * wide : s * wide + 3 * head] = grads
        mean = jnp.sum(grads.astype(F32) * y_s, axis=1, keepdims=True) / width
        pull = rinv * rinv * rinv * mean
        scal = jnp.where(lane == s, rinv, scal)
        scal = jnp.where(lane == sections + s, pull, scal)
        for t in range(s):
            part = dot(grads, m_ref[t, :, s * wide : s * wide + 3 * head], ((1,), (1,)))
            bo[t] = bo[t] + rinv * part - pull * act_o[t]
    scal_ref[...] = scal


def grads_kernel(x_ref, c_ref, made_ref, scal_ref, keep_ref, w_ref, g_ref, out_ref):
    reps, rows, shard = x_ref.shape
    sections = w_ref.shape[0]
    head = w_ref.shape[2] // 4
    wide = 4 * head
    total = reps * rows
    made = made_ref[...].reshape(total, sections * wide)
    scal = scal_ref[...].reshape(total, head)
    act = x_ref[...].reshape(total, shard).astype(F32)
    acts = []
    over = ((0,), (0,))
    for s in range(sections):
        acts.append(act)
        rinv = scal[:, s : s + 1]
        normed = (act * rinv * g_ref[s]).astype(BF16)
        grads = made[:, s * wide : s * wide + 3 * head]
        out_ref[s, :, 0 : 3 * head] = dot(normed, grads, over).astype(BF16)
        if s + 1 < sections:
            heads = made[:, s * wide + 3 * head : (s + 1) * wide]
            push = dot(heads, w_ref[s, :, 3 * head :], ((1,), (1,)))
            act = (act + keep_ref[:, s : s + 1] * push).astype(BF16).astype(F32)
    back = c_ref[...].reshape(total, shard).astype(F32)
    for s in range(sections - 1, -1, -1):
        grad_rows = (keep_ref[:, s : s + 1] * back).astype(BF16)
        heads = made[:, s * wide + 3 * head : (s + 1) * wide]
        out_ref[s, :, 3 * head :] = dot(grad_rows, heads, over).astype(BF16)
        if s > 0:
            rinv = scal[:, s : s + 1]
            pull = scal[:, sections + s : sections + s + 1]
            grads = made[:, s * wide : s * wide + 3 * head]
            d_normed = dot(grads, w_ref[s, :, 0 : 3 * head], ((1,), (1,)))
            back = back + rinv * (d_normed * g_ref[s]) - pull * acts[s]
            back = back.astype(BF16).astype(F32)


def local_call(kernel, shapes, *arrays):
    return pl.pallas_call(
        kernel,
        out_shape=shapes,
        in_specs=vmem_specs(len(arrays)),
        out_specs=vmem_specs(len(shapes)),
        compiler_params=pltpu.CompilerParams(vmem_limit_bytes=VMEM_LIMIT),
    )(*arrays)


def low_rank(x_in, cot, w_q, w_k, w_v, w_out, gains, offsets, counts):
    sections = lax.axis_size("section")
    reps = lax.axis_size("rep")
    section_pos = lax.axis_index("section")
    rep_pos = lax.axis_index("rep")
    width = x_in.shape[1]
    shard, head = w_q.shape[1:]
    batches = MB // sections
    rows = batches * ROWS
    wide = 4 * head
    x_own = lax.dynamic_slice_in_dim(x_in, section_pos * rows, rows, 0)
    c_own = lax.dynamic_slice_in_dim(cot, section_pos * rows, rows, 0)
    x_split = x_own.reshape(rows, reps, shard).swapaxes(0, 1)
    c_split = c_own.reshape(rows, reps, shard).swapaxes(0, 1)
    w_pack = jnp.concatenate([w_q[0], w_k[0], w_v[0], w_out[0]], axis=1)
    g_own = lax.dynamic_slice_in_dim(gains, rep_pos * shard, shard, 1)
    running = jnp.zeros_like(offsets[0])
    landed = []
    for s in range(sections):
        running = running + offsets[s]
        landed.append(running % reps)
    landed = jnp.stack(landed)
    my_batches = lax.dynamic_slice_in_dim(landed, section_pos * batches, batches, 1)
    rep_ids = jnp.arange(reps, dtype=jnp.int32)
    landing = (rep_ids[None, :, None] + my_batches[:, None, :]) % reps
    match = landing[..., None] == rep_ids
    allowed = jnp.sum(jnp.where(match, counts[:, None, None, :], 0), axis=-1)
    batch_ids = section_pos * batches + jnp.arange(batches, dtype=jnp.int32)
    keep = (batch_ids < allowed).astype(F32)
    keep = jnp.transpose(keep, (1, 2, 0))
    keep = jnp.broadcast_to(keep[:, :, None, :], (reps, batches, ROWS, sections))
    keep = keep.reshape(reps * rows, sections)
    keep_own = lax.dynamic_slice_in_dim(keep, rep_pos * rows, rows, 0)
    x_shard, c_shard, w_all, g_all = exchange(
        [
            (x_split, "rep", True),
            (c_split, "rep", True),
            (w_pack, "section", False),
            (g_own, "section", False),
        ],
        0,
    )
    zx, zc = local_call(
        project_kernel,
        [
            jax.ShapeDtypeStruct((reps, rows + head // reps, sections * wide), BF16),
            jax.ShapeDtypeStruct((reps, rows, sections * head), BF16),
        ],
        x_shard,
        c_shard,
        w_out[0].T,
        w_all,
        g_all,
    )
    zx, zc = exchange([(zx, "rep", True), (zc, "rep", True)], 1)
    mixed = jnp.sum(zx[:, rows:, :].astype(F32), axis=0).astype(BF16)
    (mixed,) = exchange([(mixed, "rep", False)], 2)
    (mixed,) = exchange([(mixed.reshape(head, sections * wide), "section", False)], 3)
    made, scal = local_call(
        functools.partial(chain_kernel, head ** (-0.5)),
        [
            jax.ShapeDtypeStruct((rows, sections * wide), BF16),
            jax.ShapeDtypeStruct((rows, head), F32),
        ],
        x_own,
        zx,
        zc,
        mixed,
        keep_own,
    )
    made, scal = exchange([(made, "rep", False), (scal, "rep", False)], 4)
    (parts,) = local_call(
        grads_kernel,
        [jax.ShapeDtypeStruct((sections, shard, wide), BF16)],
        x_shard,
        c_shard,
        made,
        scal,
        keep,
        w_all,
        g_all,
    )
    (parts,) = exchange([(parts, "section", True)], 5)
    total = jnp.sum(parts.astype(F32), axis=0)
    return tuple(total[None, :, i * head : (i + 1) * head] for i in range(4))


def on_device(*arrays):
    sections = lax.axis_size("section")
    head = arrays[2].shape[2]
    reps = lax.axis_size("rep")
    if sections <= 4 and MB % sections == 0 and head % (16 * reps) == 0:
        return low_rank(*arrays)
    return pipelined(*arrays)


def solution(mesh):
    in_specs = (
        P("rep", None),
        P("rep", None),
        P("section", "rep", None),
        P("section", "rep", None),
        P("section", "rep", None),
        P("section", "rep", None),
        P("section", None),
        P(),
        P(),
    )
    out_specs = (
        P("section", "rep", None),
        P("section", "rep", None),
        P("section", "rep", None),
        P("section", "rep", None),
    )
    return jax.shard_map(
        on_device, mesh=mesh, in_specs=in_specs, out_specs=out_specs, check_vma=False
    )
```

```python
import functools

import jax
import jax.numpy as jnp
from jax import lax
from jax.experimental import pallas as pl
from jax.experimental.pallas import tpu as pltpu
from jax.sharding import PartitionSpec as P


MB = 8
ROWS = 16


EPSILON = 1e-05


def from_behind(block, axis, distance):
    devices = range(lax.axis_size(axis))
    route = [(i - distance, i) for i in devices if i - distance in devices]
    return lax.ppermute(block, axis, route)


def attend(query, key, scale):
    rows_here = query.shape[0]
    scores = jnp.einsum("id,jd->ij", query, key, preferred_element_type=jnp.float32) * scale
    causal = jnp.arange(rows_here)[:, None] >= jnp.arange(rows_here)[None, :]
    expo = jnp.exp(jnp.where(causal, scores, -1e30))
    return expo / jnp.sum(expo, axis=-1, keepdims=True)


def forward_layer(layer_in, gain, weights, keep):
    weight_q, weight_k, weight_v, weight_o = weights
    scale = weight_q.shape[1] ** (-0.5)
    x_float = layer_in.astype(jnp.float32)
    rinv = lax.rsqrt(jnp.mean(x_float * x_float, axis=-1, keepdims=True) + EPSILON)
    normed = (x_float * rinv * gain).astype(jnp.bfloat16)
    query = jnp.dot(normed, weight_q, preferred_element_type=jnp.float32).astype(jnp.bfloat16)
    key = jnp.dot(normed, weight_k, preferred_element_type=jnp.float32).astype(jnp.bfloat16)
    value = jnp.dot(normed, weight_v, preferred_element_type=jnp.float32).astype(jnp.bfloat16)
    probs_low = attend(query, key, scale).astype(jnp.bfloat16)
    heads = jnp.dot(probs_low, value, preferred_element_type=jnp.float32).astype(jnp.bfloat16)
    output = lax.dot_general(
        heads, weight_o, (((1,), (1,)), ((), ())), preferred_element_type=jnp.float32
    )
    result = (x_float + keep * output).astype(jnp.bfloat16)
    return (result, normed, query, key, value, heads)


def backward_layer(grad_in, layer_in, query, key, value, gain, weights, keep):
    weight_q, weight_k, weight_v, weight_o = weights
    scale = weight_q.shape[1] ** (-0.5)
    grad_float = grad_in.astype(jnp.float32)
    grad_rows = (keep * grad_float).astype(jnp.bfloat16)
    d_heads = jnp.dot(grad_rows, weight_o, preferred_element_type=jnp.float32).astype(jnp.bfloat16)
    probs = attend(query, key, scale)
    probs_low = probs.astype(jnp.bfloat16)
    d_value = jnp.einsum(
        "ij,id->jd", probs_low, d_heads, preferred_element_type=jnp.float32
    ).astype(jnp.bfloat16)
    d_probs = jnp.einsum("id,jd->ij", d_heads, value, preferred_element_type=jnp.float32)
    d_score = (probs * (d_probs - jnp.sum(probs * d_probs, axis=-1, keepdims=True)) * scale).astype(
        jnp.bfloat16
    )
    d_query = jnp.dot(d_score, key, preferred_element_type=jnp.float32).astype(jnp.bfloat16)
    d_key = jnp.einsum("ij,id->jd", d_score, query, preferred_element_type=jnp.float32).astype(
        jnp.bfloat16
    )
    contract = (((1,), (1,)), ((), ()))
    d_normed = lax.dot_general(d_query, weight_q, contract, preferred_element_type=jnp.float32)
    d_normed = d_normed + lax.dot_general(
        d_key, weight_k, contract, preferred_element_type=jnp.float32
    )
    d_normed = d_normed + lax.dot_general(
        d_value, weight_v, contract, preferred_element_type=jnp.float32
    )
    x_float = layer_in.astype(jnp.float32)
    rinv = lax.rsqrt(jnp.mean(x_float * x_float, axis=-1, keepdims=True) + EPSILON)
    scaled = d_normed * gain
    d_input = rinv * (
        scaled - x_float * rinv * rinv * jnp.mean(scaled * x_float, axis=-1, keepdims=True)
    )
    return ((grad_float + d_input).astype(jnp.bfloat16), grad_rows, d_query, d_key, d_value)


def store_slot(store, value, slot_at, is_valid):
    old_value = lax.dynamic_index_in_dim(store, slot_at, 0, keepdims=False)
    fresh = jnp.where(is_valid, value, old_value)
    return lax.dynamic_update_index_in_dim(store, fresh, slot_at, 0)


def zeros_like_all(values):
    return tuple((jnp.zeros(value.shape, value.dtype) for value in values))


def pick_slot(store, slot_at):
    return lax.dynamic_index_in_dim(store, slot_at, 0, keepdims=False)


def local_grad(left, right):
    width_left = left.shape[-1]
    width_right = right.shape[-1]
    return jnp.einsum(
        "td,th->dh",
        left.reshape(-1, width_left),
        right.reshape(-1, width_right),
        preferred_element_type=jnp.float32,
    )


def pipelined(x_in, cot, w_q, w_k, w_v, w_out, gains, offsets, counts):
    section_count = lax.axis_size("section")
    rep_count = lax.axis_size("rep")
    section_pos = lax.axis_index("section")
    rep_pos = lax.axis_index("rep")
    weights = (
        lax.all_gather(w_q[0], "rep", axis=0, tiled=True),
        lax.all_gather(w_k[0], "rep", axis=0, tiled=True),
        lax.all_gather(w_v[0], "rep", axis=0, tiled=True),
        lax.all_gather(w_out[0], "rep", axis=0, tiled=True),
    )
    width = weights[0].shape[0]
    head_size = weights[0].shape[1]
    gain = gains[0]
    landing_sum = jnp.cumsum(offsets, axis=0) % rep_count
    my_offsets = lax.dynamic_index_in_dim(landing_sum, section_pos, 0, keepdims=False)
    landing = (rep_pos + my_offsets) % rep_count
    count_row = lax.dynamic_index_in_dim(counts, section_pos, 0, keepdims=False)
    match_rep = landing[:, None] == jnp.arange(rep_count, dtype=jnp.int32)[None, :]
    allowed = jnp.sum(jnp.where(match_rep, count_row[None, :], 0), axis=1)
    keeps = (jnp.arange(MB, dtype=jnp.int32) < allowed).astype(jnp.float32)
    inputs = x_in.reshape(MB, ROWS, width)
    top_grads = cot.reshape(MB, ROWS, width)
    tick_count = section_count + MB - 1
    row_block = jnp.zeros((ROWS, width), jnp.bfloat16)
    head_block = jnp.zeros((ROWS, head_size), jnp.bfloat16)

    def forward_tick(tick_no, carry):
        inbox, saved_in, saved_normed, saved_q, saved_k, saved_v, saved_heads = carry
        batch_pos = tick_no - section_pos
        is_valid = (batch_pos >= 0) & (batch_pos < MB)
        batch_at = jnp.clip(batch_pos, 0, MB - 1)
        own_rows = pick_slot(inputs, batch_at)
        layer_in = jnp.where(section_pos == 0, own_rows, inbox)
        keep = pick_slot(keeps, batch_at)
        blank = (row_block, row_block, head_block, head_block, head_block, head_block)
        made = lax.cond(
            is_valid,
            lambda rows_in: forward_layer(rows_in, gain, weights, keep),
            lambda rows_in: zeros_like_all(blank),
            layer_in,
        )
        result, normed, query, key, value, heads = made
        saved_in = store_slot(saved_in, layer_in, batch_at, is_valid)
        saved_normed = store_slot(saved_normed, normed, batch_at, is_valid)
        saved_q = store_slot(saved_q, query, batch_at, is_valid)
        saved_k = store_slot(saved_k, key, batch_at, is_valid)
        saved_v = store_slot(saved_v, value, batch_at, is_valid)
        saved_heads = store_slot(saved_heads, heads, batch_at, is_valid)
        inbox = from_behind(result, "section", 1)
        return (inbox, saved_in, saved_normed, saved_q, saved_k, saved_v, saved_heads)

    wide_store = jnp.zeros((MB, ROWS, width), jnp.bfloat16)
    head_store = jnp.zeros((MB, ROWS, head_size), jnp.bfloat16)
    start_fwd = (row_block, wide_store, wide_store, head_store, head_store, head_store, head_store)
    _, saved_in, saved_normed, saved_q, saved_k, saved_v, saved_heads = lax.fori_loop(
        0, tick_count, forward_tick, start_fwd
    )

    def backward_tick(tick_no, carry):
        inbox, saved_rows, saved_dq, saved_dk, saved_dv = carry
        batch_pos = tick_no - (section_count - 1 - section_pos)
        is_valid = (batch_pos >= 0) & (batch_pos < MB)
        batch_at = jnp.clip(batch_pos, 0, MB - 1)
        grad_in = jnp.where(section_pos == section_count - 1, pick_slot(top_grads, batch_at), inbox)
        layer_in = pick_slot(saved_in, batch_at)
        query = pick_slot(saved_q, batch_at)
        key = pick_slot(saved_k, batch_at)
        value = pick_slot(saved_v, batch_at)
        keep = pick_slot(keeps, batch_at)
        blank = (row_block, row_block, head_block, head_block, head_block)
        made = lax.cond(
            is_valid,
            lambda rows_in: backward_layer(
                rows_in, layer_in, query, key, value, gain, weights, keep
            ),
            lambda rows_in: zeros_like_all(blank),
            grad_in,
        )
        grad_back, grad_rows, d_query, d_key, d_value = made
        saved_rows = store_slot(saved_rows, grad_rows, batch_at, is_valid)
        saved_dq = store_slot(saved_dq, d_query, batch_at, is_valid)
        saved_dk = store_slot(saved_dk, d_key, batch_at, is_valid)
        saved_dv = store_slot(saved_dv, d_value, batch_at, is_valid)
        inbox = from_behind(grad_back, "section", -1)
        return (inbox, saved_rows, saved_dq, saved_dk, saved_dv)

    start_bwd = (row_block, wide_store, head_store, head_store, head_store)
    _, saved_rows, saved_dq, saved_dk, saved_dv = lax.fori_loop(
        0, tick_count, backward_tick, start_bwd
    )
    full_q = local_grad(saved_normed, saved_dq)
    full_k = local_grad(saved_normed, saved_dk)
    full_v = local_grad(saved_normed, saved_dv)
    full_o = local_grad(saved_rows, saved_heads)
    share_width = width // rep_count
    totals = (
        lax.psum(full_q.astype(jnp.bfloat16), "rep").astype(jnp.float32),
        lax.psum(full_k.astype(jnp.bfloat16), "rep").astype(jnp.float32),
        lax.psum(full_v.astype(jnp.bfloat16), "rep").astype(jnp.float32),
        lax.psum(full_o.astype(jnp.bfloat16), "rep").astype(jnp.float32),
    )
    parts = tuple(
        (lax.dynamic_slice_in_dim(total, rep_pos * share_width, share_width, 0) for total in totals)
    )
    return (parts[0][None], parts[1][None], parts[2][None], parts[3][None])


F32 = jnp.float32
BF16 = jnp.bfloat16
VMEM_LIMIT = 60 * 1024 * 1024


def vmem_specs(count):
    return [pl.BlockSpec(memory_space=pltpu.VMEM)] * count


def slot(axis, index, size):
    if axis == "rep":
        return lax.rem(index, 2) * (size // 2) + index // 2
    return index


MESH_ID = pl.DeviceIdType.MESH


def remote(src, dst, send, recv, target):
    return pltpu.make_async_remote_copy(
        src_ref=src, dst_ref=dst, send_sem=send, recv_sem=recv, device_id=target,
        device_id_type=MESH_ID,
    )


def greet(targets):
    barrier = pltpu.get_barrier_semaphore()
    for target in targets:
        pl.semaphore_signal(barrier, inc=1, device_id=target, device_id_type=MESH_ID)
    pl.semaphore_wait(barrier, len(targets))


def place(chips, sections):
    rep_pos = lax.axis_index("rep")
    core, chip = lax.rem(rep_pos, 2), rep_pos // 2
    section = lax.axis_index("section")
    partner = {"rep": chip * 2 + 1 - core}
    along = []
    for step in range(1, chips):
        to, source = lax.rem(chip + step, chips), lax.rem(chip + chips - step, chips)
        along.append((step, to, source, {"rep": to * 2 + core}))
    across = []
    for step in range(1, sections):
        to = lax.rem(section + step, sections)
        source = lax.rem(section + sections - step, sections)
        across.append((step, to, source, {"section": to}))
    return core, chip, section, partner, along, across


def reduce_kernel(
    z_ref, m_ref, z_land, m_out, z_core, m_core, z_sum, m_sum, m_land, m_total,
    core_send, core_recv, z_send, z_recv, m_send, m_recv, g_send, g_recv, s_send, s_recv,
):
    chips, sections = z_land.shape[0], m_out.shape[1]
    core, chip, section, partner, along, across = place(chips, sections)
    greet([partner] + [a[3] for a in along] + [a[3] for a in across])
    other = 1 - core
    m_first = remote(m_ref.at[other], m_core, core_send.at[0], core_recv.at[0], partner)
    m_first.start()
    z_first = remote(z_ref.at[other], z_core, core_send.at[1], core_recv.at[1], partner)
    z_first.start()
    m_first.wait()
    m_sum[...] = (m_ref[core].astype(F32) + m_core[...].astype(F32)).astype(BF16)
    m_copies = []
    for step, to, source, target in along:
        copy = remote(m_sum.at[to], m_land.at[step], m_send.at[step], m_recv.at[step], target)
        copy.start()
        m_copies.append(copy)
    total = m_sum[chip].astype(F32)
    z_first.wait()
    z_sum[...] = (z_ref[core].astype(F32) + z_core[...].astype(F32)).astype(BF16)
    for copy, (step, to, source, target) in zip(m_copies, along):
        copy.wait()
        total = total + m_land[step].astype(F32)
    m_total[...] = total.astype(BF16)
    spread = []
    for step, to, source, target in along:
        copy = remote(
            m_total, m_out.at[core, section, chip], g_send.at[step], g_recv.at[step], target
        )
        copy.start()
        spread.append(copy)
    z_copies = []
    for step, to, source, target in along:
        copy = remote(z_sum.at[to], z_land.at[step], z_send.at[step], z_recv.at[step], target)
        copy.start()
        z_copies.append(copy)
    m_out[core, section, chip] = total.astype(BF16)
    z_land[0] = z_sum[chip]
    for copy, (step, to, source, target) in zip(spread, along):
        copy.wait_send()
        at = m_out.at[core, section, source]
        remote(at, at, g_send.at[step], g_recv.at[step], target).wait_recv()
    mine = m_out.at[core, section]
    cross = []
    for step, to, source, target in across:
        copy = remote(mine, mine, s_send.at[step], s_recv.at[step], target)
        copy.start()
        cross.append(copy)
    own = remote(mine, mine, core_send.at[2], core_recv.at[2], partner)
    own.start()
    last = []
    for copy, (step, to, source, target) in zip(cross, across):
        at = m_out.at[core, source]
        remote(at, at, s_send.at[step], s_recv.at[step], target).wait_recv()
        copy = remote(at, at, core_send.at[2 + step], core_recv.at[2 + step], partner)
        copy.start()
        last.append(copy)
    for copy in z_copies:
        copy.wait()
    for copy in cross:
        copy.wait_send()
    own.wait_send()
    at = m_out.at[other, section]
    remote(at, at, core_send.at[2], core_recv.at[2], partner).wait_recv()
    for copy, (step, to, source, target) in zip(last, across):
        copy.wait_send()
        at = m_out.at[other, source]
        remote(at, at, core_send.at[2 + step], core_recv.at[2 + step], partner).wait_recv()


def reduce_call(z, m, sections, collective_id):
    two, chips = z.shape[:2]
    block, mix = z.shape[2:], m.shape[2:]
    dma = pltpu.SemaphoreType.DMA
    return pl.pallas_call(
        reduce_kernel,
        out_shape=[
            jax.ShapeDtypeStruct((chips,) + block, BF16),
            jax.ShapeDtypeStruct((two, sections, chips) + mix, BF16),
        ],
        in_specs=vmem_specs(2),
        out_specs=vmem_specs(2),
        scratch_shapes=[
            pltpu.VMEM((chips,) + block, BF16),
            pltpu.VMEM((chips,) + mix, BF16),
            pltpu.VMEM((chips,) + block, BF16),
            pltpu.VMEM((chips,) + mix, BF16),
            pltpu.VMEM((chips,) + mix, BF16),
            pltpu.VMEM(mix, BF16),
            dma((2 + sections,)), dma((2 + sections,)),
            dma((chips,)), dma((chips,)), dma((chips,)), dma((chips,)),
            dma((chips,)), dma((chips,)), dma((sections,)), dma((sections,)),
        ],
        compiler_params=pltpu.CompilerParams(
            collective_id=collective_id, has_side_effects=True, vmem_limit_bytes=VMEM_LIMIT
        ),
    )(z, m)


def gather_kernel(a_ref, b_ref, a_out, b_out, core_send, core_recv, z_send, z_recv):
    chips = a_out.shape[1]
    core, chip, section, partner, along, across = place(chips, 1)
    greet([partner] + [a[3] for a in along])
    other = 1 - core
    outs = ((a_ref, a_out), (b_ref, b_out))
    sends = []
    for step, to, source, target in along:
        for i, (ref, out) in enumerate(outs):
            copy = remote(
                ref, out.at[core, chip], z_send.at[i, step], z_recv.at[i, step], target
            )
            copy.start()
            sends.append(copy)
    for i, (ref, out) in enumerate(outs):
        copy = remote(ref, out.at[core, chip], core_send.at[i, 0], core_recv.at[i, 0], partner)
        copy.start()
        sends.append(copy)
        out[core, chip] = ref[...]
    for step, to, source, target in along:
        for i, (ref, out) in enumerate(outs):
            at = out.at[core, source]
            remote(at, at, z_send.at[i, step], z_recv.at[i, step], target).wait_recv()
            copy = remote(at, at, core_send.at[i, step], core_recv.at[i, step], partner)
            copy.start()
            sends.append(copy)
    for copy in sends:
        copy.wait_send()
    for step, source in [(0, chip)] + [(a[0], a[2]) for a in along]:
        for i, (ref, out) in enumerate(outs):
            at = out.at[other, source]
            remote(at, at, core_send.at[i, step], core_recv.at[i, step], partner).wait_recv()


def gather_call(a, b, chips, collective_id):
    dma = pltpu.SemaphoreType.DMA
    return pl.pallas_call(
        gather_kernel,
        out_shape=[jax.ShapeDtypeStruct((2, chips) + v.shape, v.dtype) for v in (a, b)],
        in_specs=vmem_specs(2),
        out_specs=vmem_specs(2),
        scratch_shapes=[dma((2, chips)) for _ in range(4)],
        compiler_params=pltpu.CompilerParams(
            collective_id=collective_id, has_side_effects=True, vmem_limit_bytes=VMEM_LIMIT
        ),
    )(a, b)


def exchange_kernel(plan, axes, *refs):
    count = len(plan)
    ins, outs = refs[:count], refs[count : 2 * count]
    sems = refs[2 * count :]
    barrier = pltpu.get_barrier_semaphore()
    waits = 0
    for axis, size in axes:
        me = lax.axis_index(axis)
        for step in range(1, size):
            peer = lax.rem(me + step, size)
            pl.semaphore_signal(
                barrier, inc=1, device_id={axis: peer}, device_id_type=pl.DeviceIdType.MESH
            )
            waits += 1
    pl.semaphore_wait(barrier, waits)
    copies = []
    for i, (axis, size, split) in enumerate(plan):
        send, recv = sems[2 * i], sems[2 * i + 1]
        me = lax.axis_index(axis)
        for step in range(1, size):
            peer = lax.rem(me + step, size)
            copy = pltpu.make_async_remote_copy(
                src_ref=ins[i].at[peer] if split else ins[i],
                dst_ref=outs[i].at[slot(axis, me, size)],
                send_sem=send.at[step],
                recv_sem=recv.at[step],
                device_id={axis: peer},
                device_id_type=pl.DeviceIdType.MESH,
            )
            copy.start()
            copies.append((i, axis, size, split, step, copy))
    for i, (axis, size, split) in enumerate(plan):
        me = lax.axis_index(axis)
        own = ins[i].at[me] if split else ins[i]
        outs[i][slot(axis, me, size)] = own[...]
    for i, axis, size, split, step, copy in copies:
        copy.wait_send()
        me = lax.axis_index(axis)
        source = lax.rem(me + size - step, size)
        at = slot(axis, source, size)
        pltpu.make_async_remote_copy(
            src_ref=outs[i].at[at],
            dst_ref=outs[i].at[at],
            send_sem=sems[2 * i].at[step],
            recv_sem=sems[2 * i + 1].at[step],
            device_id={axis: source},
            device_id_type=pl.DeviceIdType.MESH,
        ).wait_recv()


def exchange(items, collective_id):
    plan, shapes, scratch, names = [], [], [], []
    for array, axis, split in items:
        size = lax.axis_size(axis)
        plan.append((axis, size, split))
        block = array.shape[1:] if split else array.shape
        shapes.append(jax.ShapeDtypeStruct((size,) + block, array.dtype))
        scratch += [pltpu.SemaphoreType.DMA((size,)), pltpu.SemaphoreType.DMA((size,))]
        if (axis, size) not in names:
            names.append((axis, size))
    return pl.pallas_call(
        functools.partial(exchange_kernel, tuple(plan), tuple(names)),
        out_shape=shapes,
        in_specs=vmem_specs(len(items)),
        out_specs=vmem_specs(len(items)),
        scratch_shapes=scratch,
        compiler_params=pltpu.CompilerParams(
            collective_id=collective_id, has_side_effects=True, vmem_limit_bytes=VMEM_LIMIT
        ),
    )(*[array for array, _, _ in items])


def dot(left, right, dims=((1,), (0,))):
    return lax.dot_general(left, right, (dims, ((), ())), preferred_element_type=F32)


def project_kernel(x_ref, c_ref, w_ref, g_ref, z_ref, m_ref):
    reps, rows, shard = x_ref.shape
    sections = w_ref.shape[0]
    head = w_ref.shape[2] // 4
    qkv = 3 * head
    me = lax.axis_index("section")
    x_all = x_ref[...].reshape(reps * rows, shard)
    c_all = c_ref[...].reshape(reps * rows, shard)
    wide = x_all.astype(F32)

    def put(ref, at, block):
        shape = ref.shape[:3] + (block.shape[1],)
        ref[:, :, :, at : at + block.shape[1]] = block.astype(BF16).reshape(shape)

    for gap in range(1, sections // 2 + 1):
        far = lax.rem(me + gap, sections)
        low, high = jnp.minimum(me, far), jnp.maximum(me, far)
        turned = jnp.transpose(w_ref[low, :, qkv:].astype(F32))
        turned = (turned * g_ref[high]).astype(BF16)
        put(m_ref, (gap - 1) * qkv, dot(turned, w_ref[high, :, 0:qkv]))
    w_me = w_ref[me, :, qkv:]
    base = sections // 2 * qkv
    for s in range(sections):
        scaled = (wide * g_ref[s]).astype(BF16)
        w_o = w_ref[s, :, qkv:]
        put(z_ref, s * 4 * head, dot(scaled, w_ref[s, :, 0:qkv]))
        put(z_ref, s * 4 * head + qkv, dot(x_all, w_o))
        put(z_ref, (sections * 4 + s) * head, dot(c_all, w_o))
        put(m_ref, base + s * head, dot(w_me, w_o, ((0,), (0,))))


def chain_kernel(scale, x_ref, z_ref, m_ref, keep_ref, out_ref, scal_ref):
    sections = keep_ref.shape[1]
    head = scal_ref.shape[1]
    rows, width = x_ref.shape
    wide = 4 * head
    x_float = x_ref[...].astype(F32)
    square = jnp.sum(x_float * x_float, axis=1, keepdims=True)
    z = jnp.sum(z_ref[...].astype(F32), axis=0)
    back = z[:, sections * wide :]
    base = sections // 2 * 3 * head
    mix = [
        jnp.concatenate([m_ref[c, s].reshape(head // 2, -1) for c in range(2)], axis=0)
        for s in range(sections)
    ]

    def pair(low, high):
        gap = high - low
        owner = low
        if gap > sections // 2:
            owner, gap = high, sections - gap
        return mix[owner][:, (gap - 1) * 3 * head : gap * 3 * head]

    row = lax.broadcasted_iota(jnp.int32, (rows, rows), 0)
    col = lax.broadcasted_iota(jnp.int32, (rows, rows), 1)
    allowed = (row >= col) & (row // ROWS == col // ROWS)
    y = [z[:, s * wide : s * wide + 3 * head] for s in range(sections)]
    acto = [z[:, s * wide + 3 * head : (s + 1) * wide] for s in range(sections)]
    saved = []
    for s in range(sections):
        keep = keep_ref[:, s : s + 1]
        rinv = lax.rsqrt(jnp.maximum(square, 0.0) / width + EPSILON)
        qkv = (y[s] * rinv).astype(BF16)
        query, key, value = qkv[:, 0:head], qkv[:, head : 2 * head], qkv[:, 2 * head :]
        scores = dot(query, key, ((1,), (1,))) * scale
        expo = jnp.exp(jnp.where(allowed, scores, -1e30))
        probs = expo / jnp.sum(expo, axis=1, keepdims=True)
        low = probs.astype(BF16)
        heads = dot(low, value).astype(BF16)
        kept = heads.astype(F32) * keep
        kept_low = kept.astype(BF16)
        saved.append((rinv, query, key, value, probs, low, acto[:], y[s]))
        out_ref[:, s * wide + 3 * head : (s + 1) * wide] = heads
        moved = dot(kept_low, mix[s][:, base:])
        square = square + jnp.sum(
            kept * (2.0 * acto[s] + moved[:, s * head : (s + 1) * head]),
            axis=1,
            keepdims=True,
        )
        for t in range(sections):
            if t > s:
                y[t] = y[t] + dot(kept_low, pair(s, t))
            acto[t] = acto[t] + moved[:, t * head : (t + 1) * head]
    bo = [back[:, s * head : (s + 1) * head] for s in range(sections)]
    lane = lax.broadcasted_iota(jnp.int32, (rows, head), 1)
    scal = jnp.zeros((rows, head), F32)
    for s in range(sections - 1, -1, -1):
        keep = keep_ref[:, s : s + 1]
        rinv, query, key, value, probs, low, act_o, y_s = saved[s]
        d_heads = (keep * bo[s]).astype(BF16)
        d_value = dot(low, d_heads, ((0,), (0,))).astype(BF16)
        d_probs = dot(d_heads, value, ((1,), (1,)))
        d_score = (
            probs * (d_probs - jnp.sum(probs * d_probs, axis=1, keepdims=True)) * scale
        ).astype(BF16)
        d_query = dot(d_score, key).astype(BF16)
        d_key = dot(d_score, query, ((0,), (0,))).astype(BF16)
        grads = jnp.concatenate([d_query, d_key, d_value], axis=1)
        out_ref[:, s * wide : s * wide + 3 * head] = grads
        mean = jnp.sum(grads.astype(F32) * y_s, axis=1, keepdims=True) / width
        pull = rinv * rinv * rinv * mean
        scal = jnp.where(lane == s, rinv, scal)
        scal = jnp.where(lane == sections + s, pull, scal)
        for t in range(s):
            part = dot(grads, pair(t, s), ((1,), (1,)))
            bo[t] = bo[t] + rinv * part - pull * act_o[t]
    scal_ref[...] = scal


def grads_kernel(x_ref, c_ref, made_ref, scal_ref, keep_ref, w_ref, g_ref, out_ref):
    reps, rows, shard = x_ref.shape
    sections = w_ref.shape[0]
    head = w_ref.shape[2] // 4
    wide = 4 * head
    total = reps * rows
    made = made_ref[...].reshape(total, sections * wide)
    scal = scal_ref[...].reshape(total, head)
    act = x_ref[...].reshape(total, shard).astype(F32)
    acts = []
    over = ((0,), (0,))
    for s in range(sections):
        acts.append(act)
        rinv = scal[:, s : s + 1]
        normed = (act * rinv * g_ref[s]).astype(BF16)
        grads = made[:, s * wide : s * wide + 3 * head]
        out_ref[s, :, 0 : 3 * head] = dot(normed, grads, over).astype(BF16)
        if s + 1 < sections:
            heads = made[:, s * wide + 3 * head : (s + 1) * wide]
            push = dot(heads, w_ref[s, :, 3 * head :], ((1,), (1,)))
            act = (act + keep_ref[:, s : s + 1] * push).astype(BF16).astype(F32)
    back = c_ref[...].reshape(total, shard).astype(F32)
    for s in range(sections - 1, -1, -1):
        grad_rows = (keep_ref[:, s : s + 1] * back).astype(BF16)
        heads = made[:, s * wide + 3 * head : (s + 1) * wide]
        out_ref[s, :, 3 * head :] = dot(grad_rows, heads, over).astype(BF16)
        if s > 0:
            rinv = scal[:, s : s + 1]
            pull = scal[:, sections + s : sections + s + 1]
            grads = made[:, s * wide : s * wide + 3 * head]
            d_normed = dot(grads, w_ref[s, :, 0 : 3 * head], ((1,), (1,)))
            back = back + rinv * (d_normed * g_ref[s]) - pull * acts[s]
            back = back.astype(BF16).astype(F32)


def local_call(kernel, shapes, *arrays):
    return pl.pallas_call(
        kernel,
        out_shape=shapes,
        in_specs=vmem_specs(len(arrays)),
        out_specs=vmem_specs(len(shapes)),
        compiler_params=pltpu.CompilerParams(vmem_limit_bytes=VMEM_LIMIT),
    )(*arrays)


def low_rank(x_in, cot, w_q, w_k, w_v, w_out, gains, offsets, counts):
    sections = lax.axis_size("section")
    reps = lax.axis_size("rep")
    section_pos = lax.axis_index("section")
    rep_pos = lax.axis_index("rep")
    width = x_in.shape[1]
    shard, head = w_q.shape[1:]
    batches = MB // sections
    chips = reps // 2
    rows = batches * ROWS
    wide = 4 * head
    x_own = lax.dynamic_slice_in_dim(x_in, section_pos * rows, rows, 0)
    c_own = lax.dynamic_slice_in_dim(cot, section_pos * rows, rows, 0)
    x_split = x_own.reshape(rows, reps, shard).swapaxes(0, 1)
    c_split = c_own.reshape(rows, reps, shard).swapaxes(0, 1)
    w_pack = jnp.concatenate([w_q[0], w_k[0], w_v[0], w_out[0]], axis=1)
    g_own = lax.dynamic_slice_in_dim(gains, rep_pos * shard, shard, 1)
    running = jnp.zeros_like(offsets[0])
    landed = []
    for s in range(sections):
        running = running + offsets[s]
        landed.append(running % reps)
    landed = jnp.stack(landed)
    my_batches = lax.dynamic_slice_in_dim(landed, section_pos * batches, batches, 1)
    rep_ids = jnp.arange(reps, dtype=jnp.int32)
    slots = (rep_ids % chips) * 2 + rep_ids // chips
    landing = (slots[None, :, None] + my_batches[:, None, :]) % reps
    match = landing[..., None] == rep_ids
    allowed = jnp.sum(jnp.where(match, counts[:, None, None, :], 0), axis=-1)
    batch_ids = section_pos * batches + jnp.arange(batches, dtype=jnp.int32)
    keep = (batch_ids < allowed).astype(F32)
    keep = jnp.transpose(keep, (1, 2, 0))
    keep = jnp.broadcast_to(keep[:, :, None, :], (reps, batches, ROWS, sections))
    keep = keep.reshape(reps * rows, sections)
    keep_own = lax.dynamic_slice_in_dim(keep, slot("rep", rep_pos, reps) * rows, rows, 0)
    x_shard, c_shard, w_all, g_all = exchange(
        [
            (x_split, "rep", True),
            (c_split, "rep", True),
            (w_pack, "section", False),
            (g_own, "section", False),
        ],
        0,
    )
    mix_width = sections // 2 * 3 * head + sections * head
    z, mixed = local_call(
        project_kernel,
        [
            jax.ShapeDtypeStruct((2, chips, rows, sections * 5 * head), BF16),
            jax.ShapeDtypeStruct((2, chips, head // reps, mix_width), BF16),
        ],
        x_shard,
        c_shard,
        w_all,
        g_all,
    )
    z, mixed = reduce_call(z, mixed, sections, 1)
    made, scal = local_call(
        functools.partial(chain_kernel, head ** (-0.5)),
        [
            jax.ShapeDtypeStruct((rows, sections * wide), BF16),
            jax.ShapeDtypeStruct((rows, head), F32),
        ],
        x_own,
        z,
        mixed,
        keep_own,
    )
    made, scal = gather_call(made, scal, chips, 2)
    (parts,) = local_call(
        grads_kernel,
        [jax.ShapeDtypeStruct((sections, shard, wide), BF16)],
        x_shard,
        c_shard,
        made,
        scal,
        keep,
        w_all,
        g_all,
    )
    (parts,) = exchange([(parts, "section", True)], 3)
    total = jnp.sum(parts.astype(F32), axis=0)
    return tuple(total[None, :, i * head : (i + 1) * head] for i in range(4))


def on_device(*arrays):
    sections = lax.axis_size("section")
    head = arrays[2].shape[2]
    reps = lax.axis_size("rep")
    if sections == 4 and reps % 2 == 0 and head % (16 * reps) == 0:
        return low_rank(*arrays)
    return pipelined(*arrays)


def solution(mesh):
    in_specs = (
        P("rep", None),
        P("rep", None),
        P("section", "rep", None),
        P("section", "rep", None),
        P("section", "rep", None),
        P("section", "rep", None),
        P("section", None),
        P(),
        P(),
    )
    out_specs = (
        P("section", "rep", None),
        P("section", "rep", None),
        P("section", "rep", None),
        P("section", "rep", None),
    )
    return jax.shard_map(
        on_device, mesh=mesh, in_specs=in_specs, out_specs=out_specs, check_vma=False
    )
```

```python
import functools

import jax
import jax.numpy as jnp
from jax import lax
from jax.experimental import pallas as pl
from jax.experimental.pallas import tpu as pltpu
from jax.sharding import PartitionSpec as P


MB = 8
ROWS = 16


EPSILON = 1e-05


def from_behind(block, axis, distance):
    devices = range(lax.axis_size(axis))
    route = [(i - distance, i) for i in devices if i - distance in devices]
    return lax.ppermute(block, axis, route)


def attend(query, key, scale):
    rows_here = query.shape[0]
    scores = jnp.einsum("id,jd->ij", query, key, preferred_element_type=jnp.float32) * scale
    causal = jnp.arange(rows_here)[:, None] >= jnp.arange(rows_here)[None, :]
    expo = jnp.exp(jnp.where(causal, scores, -1e30))
    return expo / jnp.sum(expo, axis=-1, keepdims=True)


def forward_layer(layer_in, gain, weights, keep):
    weight_q, weight_k, weight_v, weight_o = weights
    scale = weight_q.shape[1] ** (-0.5)
    x_float = layer_in.astype(jnp.float32)
    rinv = lax.rsqrt(jnp.mean(x_float * x_float, axis=-1, keepdims=True) + EPSILON)
    normed = (x_float * rinv * gain).astype(jnp.bfloat16)
    query = jnp.dot(normed, weight_q, preferred_element_type=jnp.float32).astype(jnp.bfloat16)
    key = jnp.dot(normed, weight_k, preferred_element_type=jnp.float32).astype(jnp.bfloat16)
    value = jnp.dot(normed, weight_v, preferred_element_type=jnp.float32).astype(jnp.bfloat16)
    probs_low = attend(query, key, scale).astype(jnp.bfloat16)
    heads = jnp.dot(probs_low, value, preferred_element_type=jnp.float32).astype(jnp.bfloat16)
    output = lax.dot_general(
        heads, weight_o, (((1,), (1,)), ((), ())), preferred_element_type=jnp.float32
    )
    result = (x_float + keep * output).astype(jnp.bfloat16)
    return (result, normed, query, key, value, heads)


def backward_layer(grad_in, layer_in, query, key, value, gain, weights, keep):
    weight_q, weight_k, weight_v, weight_o = weights
    scale = weight_q.shape[1] ** (-0.5)
    grad_float = grad_in.astype(jnp.float32)
    grad_rows = (keep * grad_float).astype(jnp.bfloat16)
    d_heads = jnp.dot(grad_rows, weight_o, preferred_element_type=jnp.float32).astype(jnp.bfloat16)
    probs = attend(query, key, scale)
    probs_low = probs.astype(jnp.bfloat16)
    d_value = jnp.einsum(
        "ij,id->jd", probs_low, d_heads, preferred_element_type=jnp.float32
    ).astype(jnp.bfloat16)
    d_probs = jnp.einsum("id,jd->ij", d_heads, value, preferred_element_type=jnp.float32)
    d_score = (probs * (d_probs - jnp.sum(probs * d_probs, axis=-1, keepdims=True)) * scale).astype(
        jnp.bfloat16
    )
    d_query = jnp.dot(d_score, key, preferred_element_type=jnp.float32).astype(jnp.bfloat16)
    d_key = jnp.einsum("ij,id->jd", d_score, query, preferred_element_type=jnp.float32).astype(
        jnp.bfloat16
    )
    contract = (((1,), (1,)), ((), ()))
    d_normed = lax.dot_general(d_query, weight_q, contract, preferred_element_type=jnp.float32)
    d_normed = d_normed + lax.dot_general(
        d_key, weight_k, contract, preferred_element_type=jnp.float32
    )
    d_normed = d_normed + lax.dot_general(
        d_value, weight_v, contract, preferred_element_type=jnp.float32
    )
    x_float = layer_in.astype(jnp.float32)
    rinv = lax.rsqrt(jnp.mean(x_float * x_float, axis=-1, keepdims=True) + EPSILON)
    scaled = d_normed * gain
    d_input = rinv * (
        scaled - x_float * rinv * rinv * jnp.mean(scaled * x_float, axis=-1, keepdims=True)
    )
    return ((grad_float + d_input).astype(jnp.bfloat16), grad_rows, d_query, d_key, d_value)


def store_slot(store, value, slot_at, is_valid):
    old_value = lax.dynamic_index_in_dim(store, slot_at, 0, keepdims=False)
    fresh = jnp.where(is_valid, value, old_value)
    return lax.dynamic_update_index_in_dim(store, fresh, slot_at, 0)


def zeros_like_all(values):
    return tuple((jnp.zeros(value.shape, value.dtype) for value in values))


def pick_slot(store, slot_at):
    return lax.dynamic_index_in_dim(store, slot_at, 0, keepdims=False)


def local_grad(left, right):
    width_left = left.shape[-1]
    width_right = right.shape[-1]
    return jnp.einsum(
        "td,th->dh",
        left.reshape(-1, width_left),
        right.reshape(-1, width_right),
        preferred_element_type=jnp.float32,
    )


def pipelined(x_in, cot, w_q, w_k, w_v, w_out, gains, offsets, counts):
    section_count = lax.axis_size("section")
    rep_count = lax.axis_size("rep")
    section_pos = lax.axis_index("section")
    rep_pos = lax.axis_index("rep")
    weights = (
        lax.all_gather(w_q[0], "rep", axis=0, tiled=True),
        lax.all_gather(w_k[0], "rep", axis=0, tiled=True),
        lax.all_gather(w_v[0], "rep", axis=0, tiled=True),
        lax.all_gather(w_out[0], "rep", axis=0, tiled=True),
    )
    width = weights[0].shape[0]
    head_size = weights[0].shape[1]
    gain = gains[0]
    landing_sum = jnp.cumsum(offsets, axis=0) % rep_count
    my_offsets = lax.dynamic_index_in_dim(landing_sum, section_pos, 0, keepdims=False)
    landing = (rep_pos + my_offsets) % rep_count
    count_row = lax.dynamic_index_in_dim(counts, section_pos, 0, keepdims=False)
    match_rep = landing[:, None] == jnp.arange(rep_count, dtype=jnp.int32)[None, :]
    allowed = jnp.sum(jnp.where(match_rep, count_row[None, :], 0), axis=1)
    keeps = (jnp.arange(MB, dtype=jnp.int32) < allowed).astype(jnp.float32)
    inputs = x_in.reshape(MB, ROWS, width)
    top_grads = cot.reshape(MB, ROWS, width)
    tick_count = section_count + MB - 1
    row_block = jnp.zeros((ROWS, width), jnp.bfloat16)
    head_block = jnp.zeros((ROWS, head_size), jnp.bfloat16)

    def forward_tick(tick_no, carry):
        inbox, saved_in, saved_normed, saved_q, saved_k, saved_v, saved_heads = carry
        batch_pos = tick_no - section_pos
        is_valid = (batch_pos >= 0) & (batch_pos < MB)
        batch_at = jnp.clip(batch_pos, 0, MB - 1)
        own_rows = pick_slot(inputs, batch_at)
        layer_in = jnp.where(section_pos == 0, own_rows, inbox)
        keep = pick_slot(keeps, batch_at)
        blank = (row_block, row_block, head_block, head_block, head_block, head_block)
        made = lax.cond(
            is_valid,
            lambda rows_in: forward_layer(rows_in, gain, weights, keep),
            lambda rows_in: zeros_like_all(blank),
            layer_in,
        )
        result, normed, query, key, value, heads = made
        saved_in = store_slot(saved_in, layer_in, batch_at, is_valid)
        saved_normed = store_slot(saved_normed, normed, batch_at, is_valid)
        saved_q = store_slot(saved_q, query, batch_at, is_valid)
        saved_k = store_slot(saved_k, key, batch_at, is_valid)
        saved_v = store_slot(saved_v, value, batch_at, is_valid)
        saved_heads = store_slot(saved_heads, heads, batch_at, is_valid)
        inbox = from_behind(result, "section", 1)
        return (inbox, saved_in, saved_normed, saved_q, saved_k, saved_v, saved_heads)

    wide_store = jnp.zeros((MB, ROWS, width), jnp.bfloat16)
    head_store = jnp.zeros((MB, ROWS, head_size), jnp.bfloat16)
    start_fwd = (row_block, wide_store, wide_store, head_store, head_store, head_store, head_store)
    _, saved_in, saved_normed, saved_q, saved_k, saved_v, saved_heads = lax.fori_loop(
        0, tick_count, forward_tick, start_fwd
    )

    def backward_tick(tick_no, carry):
        inbox, saved_rows, saved_dq, saved_dk, saved_dv = carry
        batch_pos = tick_no - (section_count - 1 - section_pos)
        is_valid = (batch_pos >= 0) & (batch_pos < MB)
        batch_at = jnp.clip(batch_pos, 0, MB - 1)
        grad_in = jnp.where(section_pos == section_count - 1, pick_slot(top_grads, batch_at), inbox)
        layer_in = pick_slot(saved_in, batch_at)
        query = pick_slot(saved_q, batch_at)
        key = pick_slot(saved_k, batch_at)
        value = pick_slot(saved_v, batch_at)
        keep = pick_slot(keeps, batch_at)
        blank = (row_block, row_block, head_block, head_block, head_block)
        made = lax.cond(
            is_valid,
            lambda rows_in: backward_layer(
                rows_in, layer_in, query, key, value, gain, weights, keep
            ),
            lambda rows_in: zeros_like_all(blank),
            grad_in,
        )
        grad_back, grad_rows, d_query, d_key, d_value = made
        saved_rows = store_slot(saved_rows, grad_rows, batch_at, is_valid)
        saved_dq = store_slot(saved_dq, d_query, batch_at, is_valid)
        saved_dk = store_slot(saved_dk, d_key, batch_at, is_valid)
        saved_dv = store_slot(saved_dv, d_value, batch_at, is_valid)
        inbox = from_behind(grad_back, "section", -1)
        return (inbox, saved_rows, saved_dq, saved_dk, saved_dv)

    start_bwd = (row_block, wide_store, head_store, head_store, head_store)
    _, saved_rows, saved_dq, saved_dk, saved_dv = lax.fori_loop(
        0, tick_count, backward_tick, start_bwd
    )
    full_q = local_grad(saved_normed, saved_dq)
    full_k = local_grad(saved_normed, saved_dk)
    full_v = local_grad(saved_normed, saved_dv)
    full_o = local_grad(saved_rows, saved_heads)
    share_width = width // rep_count
    totals = (
        lax.psum(full_q.astype(jnp.bfloat16), "rep").astype(jnp.float32),
        lax.psum(full_k.astype(jnp.bfloat16), "rep").astype(jnp.float32),
        lax.psum(full_v.astype(jnp.bfloat16), "rep").astype(jnp.float32),
        lax.psum(full_o.astype(jnp.bfloat16), "rep").astype(jnp.float32),
    )
    parts = tuple(
        (lax.dynamic_slice_in_dim(total, rep_pos * share_width, share_width, 0) for total in totals)
    )
    return (parts[0][None], parts[1][None], parts[2][None], parts[3][None])


F32 = jnp.float32
BF16 = jnp.bfloat16
VMEM_LIMIT = 60 * 1024 * 1024


def vmem_specs(count):
    return [pl.BlockSpec(memory_space=pltpu.VMEM)] * count


def slot(axis, index, size):
    if axis == "rep":
        return lax.rem(index, 2) * (size // 2) + index // 2
    return index


MESH_ID = pl.DeviceIdType.MESH


def remote(src, dst, send, recv, target):
    return pltpu.make_async_remote_copy(
        src_ref=src, dst_ref=dst, send_sem=send, recv_sem=recv, device_id=target,
        device_id_type=MESH_ID,
    )


def greet(targets):
    barrier = pltpu.get_barrier_semaphore()
    for target in targets:
        pl.semaphore_signal(barrier, inc=1, device_id=target, device_id_type=MESH_ID)
    pl.semaphore_wait(barrier, len(targets))


def place(chips, sections):
    rep_pos = lax.axis_index("rep")
    core, chip = lax.rem(rep_pos, 2), rep_pos // 2
    section = lax.axis_index("section")
    partner = {"rep": chip * 2 + 1 - core}
    along = []
    for step in range(1, chips):
        to, source = lax.rem(chip + step, chips), lax.rem(chip + chips - step, chips)
        along.append((step, to, source, {"rep": to * 2 + core}))
    across = []
    for step in range(1, sections):
        to = lax.rem(section + step, sections)
        source = lax.rem(section + sections - step, sections)
        across.append((step, to, source, {"section": to}))
    return core, chip, section, partner, along, across


def reduce_kernel(
    z_ref, m_ref, z_land, m_out, z_core, m_core, z_sum, m_sum, m_land, m_total,
    core_send, core_recv, z_send, z_recv, m_send, m_recv, g_send, g_recv, s_send, s_recv,
):
    chips, sections = z_land.shape[0], m_out.shape[1]
    core, chip, section, partner, along, across = place(chips, sections)
    greet([partner] + [a[3] for a in along] + [a[3] for a in across])
    other = 1 - core
    m_first = remote(m_ref.at[other], m_core, core_send.at[0], core_recv.at[0], partner)
    m_first.start()
    z_first = remote(z_ref.at[other], z_core, core_send.at[1], core_recv.at[1], partner)
    z_first.start()
    m_first.wait()
    m_sum[...] = (m_ref[core].astype(F32) + m_core[...].astype(F32)).astype(BF16)
    m_copies = []
    for step, to, source, target in along:
        copy = remote(m_sum.at[to], m_land.at[step], m_send.at[step], m_recv.at[step], target)
        copy.start()
        m_copies.append(copy)
    total = m_sum[chip].astype(F32)
    z_first.wait()
    z_sum[...] = (z_ref[core].astype(F32) + z_core[...].astype(F32)).astype(BF16)
    for copy, (step, to, source, target) in zip(m_copies, along):
        copy.wait()
        total = total + m_land[step].astype(F32)
    m_total[...] = total.astype(BF16)
    spread = []
    for step, to, source, target in along:
        copy = remote(
            m_total, m_out.at[core, section, chip], g_send.at[step], g_recv.at[step], target
        )
        copy.start()
        spread.append(copy)
    z_copies = []
    for step, to, source, target in along:
        copy = remote(z_sum.at[to], z_land.at[step], z_send.at[step], z_recv.at[step], target)
        copy.start()
        z_copies.append(copy)
    m_out[core, section, chip] = total.astype(BF16)
    z_land[0] = z_sum[chip]
    for copy, (step, to, source, target) in zip(spread, along):
        copy.wait_send()
        at = m_out.at[core, section, source]
        remote(at, at, g_send.at[step], g_recv.at[step], target).wait_recv()
    mine = m_out.at[core, section]
    cross = []
    for step, to, source, target in across:
        copy = remote(mine, mine, s_send.at[step], s_recv.at[step], target)
        copy.start()
        cross.append(copy)
    own = remote(mine, mine, core_send.at[2], core_recv.at[2], partner)
    own.start()
    last = []
    for copy, (step, to, source, target) in zip(cross, across):
        at = m_out.at[core, source]
        remote(at, at, s_send.at[step], s_recv.at[step], target).wait_recv()
        copy = remote(at, at, core_send.at[2 + step], core_recv.at[2 + step], partner)
        copy.start()
        last.append(copy)
    for copy in z_copies:
        copy.wait()
    for copy in cross:
        copy.wait_send()
    own.wait_send()
    at = m_out.at[other, section]
    remote(at, at, core_send.at[2], core_recv.at[2], partner).wait_recv()
    for copy, (step, to, source, target) in zip(last, across):
        copy.wait_send()
        at = m_out.at[other, source]
        remote(at, at, core_send.at[2 + step], core_recv.at[2 + step], partner).wait_recv()


def reduce_call(z, m, sections, collective_id):
    two, chips = z.shape[:2]
    block, mix = z.shape[2:], m.shape[2:]
    dma = pltpu.SemaphoreType.DMA
    return pl.pallas_call(
        reduce_kernel,
        out_shape=[
            jax.ShapeDtypeStruct((chips,) + block, BF16),
            jax.ShapeDtypeStruct((two, sections, chips) + mix, BF16),
        ],
        in_specs=vmem_specs(2),
        out_specs=vmem_specs(2),
        scratch_shapes=[
            pltpu.VMEM((chips,) + block, BF16),
            pltpu.VMEM((chips,) + mix, BF16),
            pltpu.VMEM((chips,) + block, BF16),
            pltpu.VMEM((chips,) + mix, BF16),
            pltpu.VMEM((chips,) + mix, BF16),
            pltpu.VMEM(mix, BF16),
            dma((2 + sections,)), dma((2 + sections,)),
            dma((chips,)), dma((chips,)), dma((chips,)), dma((chips,)),
            dma((chips,)), dma((chips,)), dma((sections,)), dma((sections,)),
        ],
        compiler_params=pltpu.CompilerParams(
            collective_id=collective_id, has_side_effects=True, vmem_limit_bytes=VMEM_LIMIT
        ),
    )(z, m)


def exchange_kernel(plan, axes, *refs):
    count = len(plan)
    ins, outs = refs[:count], refs[count : 2 * count]
    sems = refs[2 * count :]
    barrier = pltpu.get_barrier_semaphore()
    waits = 0
    for axis, size in axes:
        me = lax.axis_index(axis)
        for step in range(1, size):
            peer = lax.rem(me + step, size)
            pl.semaphore_signal(
                barrier, inc=1, device_id={axis: peer}, device_id_type=pl.DeviceIdType.MESH
            )
            waits += 1
    pl.semaphore_wait(barrier, waits)
    copies = []
    for i, (axis, size, split) in enumerate(plan):
        send, recv = sems[2 * i], sems[2 * i + 1]
        me = lax.axis_index(axis)
        for step in range(1, size):
            peer = lax.rem(me + step, size)
            copy = pltpu.make_async_remote_copy(
                src_ref=ins[i].at[peer] if split else ins[i],
                dst_ref=outs[i].at[slot(axis, me, size)],
                send_sem=send.at[step],
                recv_sem=recv.at[step],
                device_id={axis: peer},
                device_id_type=pl.DeviceIdType.MESH,
            )
            copy.start()
            copies.append((i, axis, size, split, step, copy))
    for i, (axis, size, split) in enumerate(plan):
        me = lax.axis_index(axis)
        own = ins[i].at[me] if split else ins[i]
        outs[i][slot(axis, me, size)] = own[...]
    for i, axis, size, split, step, copy in copies:
        copy.wait_send()
        me = lax.axis_index(axis)
        source = lax.rem(me + size - step, size)
        at = slot(axis, source, size)
        pltpu.make_async_remote_copy(
            src_ref=outs[i].at[at],
            dst_ref=outs[i].at[at],
            send_sem=sems[2 * i].at[step],
            recv_sem=sems[2 * i + 1].at[step],
            device_id={axis: source},
            device_id_type=pl.DeviceIdType.MESH,
        ).wait_recv()


def exchange(items, collective_id):
    plan, shapes, scratch, names = [], [], [], []
    for array, axis, split in items:
        size = lax.axis_size(axis)
        plan.append((axis, size, split))
        block = array.shape[1:] if split else array.shape
        shapes.append(jax.ShapeDtypeStruct((size,) + block, array.dtype))
        scratch += [pltpu.SemaphoreType.DMA((size,)), pltpu.SemaphoreType.DMA((size,))]
        if (axis, size) not in names:
            names.append((axis, size))
    return pl.pallas_call(
        functools.partial(exchange_kernel, tuple(plan), tuple(names)),
        out_shape=shapes,
        in_specs=vmem_specs(len(items)),
        out_specs=vmem_specs(len(items)),
        scratch_shapes=scratch,
        compiler_params=pltpu.CompilerParams(
            collective_id=collective_id, has_side_effects=True, vmem_limit_bytes=VMEM_LIMIT
        ),
    )(*[array for array, _, _ in items])


def dot(left, right, dims=((1,), (0,))):
    return lax.dot_general(left, right, (dims, ((), ())), preferred_element_type=F32)


def project_kernel(x_ref, c_ref, w_ref, g_ref, z_ref, m_ref):
    reps, rows, shard = x_ref.shape
    sections = w_ref.shape[0]
    head = w_ref.shape[2] // 4
    qkv = 3 * head
    me = lax.axis_index("section")
    x_all = x_ref[...].reshape(reps * rows, shard)
    c_all = c_ref[...].reshape(reps * rows, shard)
    wide = x_all.astype(F32)

    def put(ref, at, block):
        shape = ref.shape[:3] + (block.shape[1],)
        ref[:, :, :, at : at + block.shape[1]] = block.astype(BF16).reshape(shape)

    for gap in range(1, sections // 2 + 1):
        far = lax.rem(me + gap, sections)
        low, high = jnp.minimum(me, far), jnp.maximum(me, far)
        turned = jnp.transpose(w_ref[low, :, qkv:].astype(F32))
        turned = (turned * g_ref[high]).astype(BF16)
        put(m_ref, (gap - 1) * qkv, dot(turned, w_ref[high, :, 0:qkv]))
    w_me = w_ref[me, :, qkv:]
    base = sections // 2 * qkv
    for s in range(sections):
        scaled = (wide * g_ref[s]).astype(BF16)
        w_o = w_ref[s, :, qkv:]
        put(z_ref, s * 4 * head, dot(scaled, w_ref[s, :, 0:qkv]))
        put(z_ref, s * 4 * head + qkv, dot(x_all, w_o))
        put(z_ref, (sections * 4 + s) * head, dot(c_all, w_o))
        put(m_ref, base + s * head, dot(w_me, w_o, ((0,), (0,))))


def chain_kernel(scale, x_ref, z_ref, m_ref, keep_ref, out_ref, scal_ref):
    sections = keep_ref.shape[1]
    head = scal_ref.shape[1]
    rows, width = x_ref.shape
    wide = 4 * head
    x_float = x_ref[...].astype(F32)
    square = jnp.sum(x_float * x_float, axis=1, keepdims=True)
    z = jnp.sum(z_ref[...].astype(F32), axis=0)
    back = z[:, sections * wide :]
    base = sections // 2 * 3 * head
    mix = [
        jnp.concatenate([m_ref[c, s].reshape(head // 2, -1) for c in range(2)], axis=0)
        for s in range(sections)
    ]

    def pair(low, high):
        gap = high - low
        owner = low
        if gap > sections // 2:
            owner, gap = high, sections - gap
        return mix[owner][:, (gap - 1) * 3 * head : gap * 3 * head]

    row = lax.broadcasted_iota(jnp.int32, (rows, rows), 0)
    col = lax.broadcasted_iota(jnp.int32, (rows, rows), 1)
    allowed = (row >= col) & (row // ROWS == col // ROWS)
    y = [z[:, s * wide : s * wide + 3 * head] for s in range(sections)]
    acto = [z[:, s * wide + 3 * head : (s + 1) * wide] for s in range(sections)]
    saved = []
    for s in range(sections):
        keep = keep_ref[:, s : s + 1]
        rinv = lax.rsqrt(jnp.maximum(square, 0.0) / width + EPSILON)
        qkv = (y[s] * rinv).astype(BF16)
        query, key, value = qkv[:, 0:head], qkv[:, head : 2 * head], qkv[:, 2 * head :]
        scores = dot(query, key, ((1,), (1,))) * scale
        expo = jnp.exp(jnp.where(allowed, scores, -1e30))
        probs = expo / jnp.sum(expo, axis=1, keepdims=True)
        low = probs.astype(BF16)
        heads = dot(low, value).astype(BF16)
        kept = heads.astype(F32) * keep
        kept_low = kept.astype(BF16)
        saved.append((rinv, query, key, value, probs, low, acto[:], y[s]))
        out_ref[0, :, s * head : (s + 1) * head] = heads
        moved = dot(kept_low, mix[s][:, base:])
        square = square + jnp.sum(
            kept * (2.0 * acto[s] + moved[:, s * head : (s + 1) * head]),
            axis=1,
            keepdims=True,
        )
        for t in range(sections):
            if t > s:
                y[t] = y[t] + dot(kept_low, pair(s, t))
            acto[t] = acto[t] + moved[:, t * head : (t + 1) * head]
    bo = [back[:, s * head : (s + 1) * head] for s in range(sections)]
    lane = lax.broadcasted_iota(jnp.int32, (rows, head), 1)
    scal = jnp.zeros((rows, head), F32)
    for s in range(sections - 1, -1, -1):
        keep = keep_ref[:, s : s + 1]
        rinv, query, key, value, probs, low, act_o, y_s = saved[s]
        d_heads = (keep * bo[s]).astype(BF16)
        d_value = dot(low, d_heads, ((0,), (0,))).astype(BF16)
        d_probs = dot(d_heads, value, ((1,), (1,)))
        d_score = (
            probs * (d_probs - jnp.sum(probs * d_probs, axis=1, keepdims=True)) * scale
        ).astype(BF16)
        d_query = dot(d_score, key).astype(BF16)
        d_key = dot(d_score, query, ((0,), (0,))).astype(BF16)
        grads = jnp.concatenate([d_query, d_key, d_value], axis=1)
        out_ref[1, :, s * head : (s + 1) * head] = d_value
        out_ref[2, :, s * head : (s + 1) * head] = d_query
        out_ref[3, :, s * head : (s + 1) * head] = d_key
        mean = jnp.sum(grads.astype(F32) * y_s, axis=1, keepdims=True) / width
        pull = rinv * rinv * rinv * mean
        scal = jnp.where(lane == s, rinv, scal)
        scal = jnp.where(lane == sections + s, pull, scal)
        for t in range(s):
            part = dot(grads, pair(t, s), ((1,), (1,)))
            bo[t] = bo[t] + rinv * part - pull * act_o[t]
    scal_ref[...] = scal


def tail_kernel(
    x_ref, c_ref, made_ref, scal_ref, keep_ref, w_ref, g_ref,
    q_out, k_out, v_out, o_out,
    made, scal, normed, acts, part, relay, from_x, from_y, merged,
    z_send, z_recv, core_send, core_recv, h_send, h_recv,
):
    reps, rows, shard = x_ref.shape
    sections = w_ref.shape[0]
    head = w_ref.shape[2] // 4
    qkv = 3 * head
    half = shard // 2
    chips = reps // 2
    total = reps * rows
    core, chip, section, partner, along, _ = place(chips, 1)
    other = 1 - core
    near_x = section + 1 - 2 * lax.rem(section, 2)
    near_y = lax.rem(section + 2, 4)
    diagonal = 3 - section
    to_x, to_y = {"section": near_x}, {"section": near_y}
    greet([partner] + [a[3] for a in along] + [to_x, to_y])
    outs = [made.at[i] for i in range(4)] + [scal]
    ins = [made_ref.at[i] for i in range(4)] + [scal_ref]
    sends = []

    def start(copy):
        copy.start()
        sends.append(copy)

    for i in (4, 0, 1, 2, 3):
        for step, to, source, target in along:
            at = outs[i].at[core, chip]
            start(remote(ins[i], at, z_send.at[i, step], z_recv.at[i, step], target))
        at = outs[i].at[core, chip]
        start(remote(ins[i], at, core_send.at[i, 0], core_recv.at[i, 0], partner))
    for i in range(4):
        made[i, core, chip] = made_ref[i]
    scal[core, chip] = scal_ref[...]

    def arrive(kinds):
        for i in kinds:
            for step, to, source, target in along:
                at = outs[i].at[core, source]
                remote(at, at, z_send.at[i, step], z_recv.at[i, step], target).wait_recv()
                start(remote(at, at, core_send.at[i, step], core_recv.at[i, step], partner))
        for i in kinds:
            for step, source in [(0, chip)] + [(a[0], a[2]) for a in along]:
                at = outs[i].at[other, source]
                remote(at, at, core_send.at[i, step], core_recv.at[i, step], partner).wait_recv()

    first, second = pl.ds(0, half), pl.ds(half, half)

    def message(kind, number, src, dst, target):
        return remote(src, dst, h_send.at[kind, number], h_recv.at[kind, number], target)

    def messages(kind):
        p = part.at[kind]
        return [
            message(kind, 0, p.at[diagonal, first], relay.at[kind, 0], to_x),
            message(kind, 1, p.at[near_x, first], from_x.at[kind, first], to_x),
            message(kind, 2, merged.at[kind, 1], from_x.at[kind, second], to_x),
            message(kind, 3, p.at[diagonal, second], relay.at[kind, 1], to_y),
            message(kind, 4, p.at[near_y, second], from_y.at[kind, second], to_y),
            message(kind, 5, merged.at[kind, 0], from_y.at[kind, first], to_y),
        ]

    def send_parts(kind):
        copies = messages(kind)
        for number in (0, 3, 1, 4):
            start(copies[number])

    def send_merged(kind):
        copies = messages(kind)
        copies[0].wait_recv()
        merged[kind, 0] = (
            relay[kind, 0].astype(F32) + part[kind, near_y, 0:half].astype(F32)
        ).astype(BF16)
        start(copies[5])
        copies[3].wait_recv()
        merged[kind, 1] = (
            relay[kind, 1].astype(F32) + part[kind, near_x, half:].astype(F32)
        ).astype(BF16)
        start(copies[2])

    def block(kind, s):
        return made[kind, :, :, :, s * head : (s + 1) * head].reshape(total, head)

    def column(at):
        return scal[:, :, :, at : at + 1].reshape(total, 1)

    over = ((0,), (0,))
    across = ((1,), (1,))
    arrive((4, 0, 1))
    act = x_ref[...].reshape(total, shard).astype(F32)
    for s in range(sections):
        acts[s] = act.astype(BF16)
        normed[s] = (act * column(s) * g_ref[s]).astype(BF16)
        part[2, s] = dot(normed[s], block(1, s), over).astype(BF16)
        if s + 1 < sections:
            push = dot(block(0, s), w_ref[s, :, qkv:], across)
            act = (act + keep_ref[:, s : s + 1] * push).astype(BF16).astype(F32)
    send_parts(2)
    arrive((2,))
    for s in range(sections):
        part[0, s] = dot(normed[s], block(2, s), over).astype(BF16)
    send_parts(0)
    arrive((3,))
    for s in range(sections):
        part[1, s] = dot(normed[s], block(3, s), over).astype(BF16)
    send_merged(2)
    send_parts(1)
    back = c_ref[...].reshape(total, shard).astype(F32)
    for s in range(sections - 1, -1, -1):
        grad_rows = (keep_ref[:, s : s + 1] * back).astype(BF16)
        part[3, s] = dot(grad_rows, block(0, s), over).astype(BF16)
        if s > 0:
            d_normed = dot(block(2, s), w_ref[s, :, 0:head], across)
            d_normed = d_normed + dot(block(3, s), w_ref[s, :, head : 2 * head], across)
            d_normed = d_normed + dot(block(1, s), w_ref[s, :, 2 * head : qkv], across)
            pull = column(sections + s)
            back = back + column(s) * (d_normed * g_ref[s]) - pull * acts[s].astype(F32)
            back = back.astype(BF16).astype(F32)
    send_merged(0)
    send_parts(3)
    send_merged(1)

    def finish(kind, out):
        copies = messages(kind)
        for number in (1, 2, 4, 5):
            copies[number].wait_recv()
        out[...] = (
            part[kind, section].astype(F32)
            + from_x[kind].astype(F32)
            + from_y[kind].astype(F32)
        )

    finish(2, v_out)
    send_merged(3)
    finish(0, q_out)
    finish(1, k_out)
    finish(3, o_out)
    for copy in sends:
        copy.wait_send()


def tail_call(x, c, made, scal, keep, w, g, collective_id):
    reps, rows, shard = x.shape
    sections = w.shape[0]
    head = w.shape[2] // 4
    total, half = reps * rows, shard // 2
    chips = reps // 2
    dma = pltpu.SemaphoreType.DMA
    return pl.pallas_call(
        tail_kernel,
        out_shape=[jax.ShapeDtypeStruct((shard, head), F32)] * 4,
        in_specs=vmem_specs(7),
        out_specs=vmem_specs(4),
        scratch_shapes=[
            pltpu.VMEM((4, 2, chips) + made.shape[1:], BF16),
            pltpu.VMEM((2, chips) + scal.shape, F32),
            pltpu.VMEM((sections, total, shard), BF16),
            pltpu.VMEM((sections, total, shard), BF16),
            pltpu.VMEM((4, sections, shard, head), BF16),
            pltpu.VMEM((4, 2, half, head), BF16),
            pltpu.VMEM((4, shard, head), BF16),
            pltpu.VMEM((4, shard, head), BF16),
            pltpu.VMEM((4, 2, half, head), BF16),
            dma((5, chips)), dma((5, chips)), dma((5, chips)), dma((5, chips)),
            dma((4, 6)), dma((4, 6)),
        ],
        compiler_params=pltpu.CompilerParams(
            collective_id=collective_id, has_side_effects=True, vmem_limit_bytes=VMEM_LIMIT
        ),
    )(x, c, made, scal, keep, w, g)


def local_call(kernel, shapes, *arrays):
    return pl.pallas_call(
        kernel,
        out_shape=shapes,
        in_specs=vmem_specs(len(arrays)),
        out_specs=vmem_specs(len(shapes)),
        compiler_params=pltpu.CompilerParams(vmem_limit_bytes=VMEM_LIMIT),
    )(*arrays)


def low_rank(x_in, cot, w_q, w_k, w_v, w_out, gains, offsets, counts):
    sections = lax.axis_size("section")
    reps = lax.axis_size("rep")
    section_pos = lax.axis_index("section")
    rep_pos = lax.axis_index("rep")
    width = x_in.shape[1]
    shard, head = w_q.shape[1:]
    batches = MB // sections
    chips = reps // 2
    rows = batches * ROWS
    wide = 4 * head
    x_own = lax.dynamic_slice_in_dim(x_in, section_pos * rows, rows, 0)
    c_own = lax.dynamic_slice_in_dim(cot, section_pos * rows, rows, 0)
    x_split = x_own.reshape(rows, reps, shard).swapaxes(0, 1)
    c_split = c_own.reshape(rows, reps, shard).swapaxes(0, 1)
    w_pack = jnp.concatenate([w_q[0], w_k[0], w_v[0], w_out[0]], axis=1)
    g_own = lax.dynamic_slice_in_dim(gains, rep_pos * shard, shard, 1)
    running = jnp.zeros_like(offsets[0])
    landed = []
    for s in range(sections):
        running = running + offsets[s]
        landed.append(running % reps)
    landed = jnp.stack(landed)
    my_batches = lax.dynamic_slice_in_dim(landed, section_pos * batches, batches, 1)
    rep_ids = jnp.arange(reps, dtype=jnp.int32)
    slots = (rep_ids % chips) * 2 + rep_ids // chips
    landing = (slots[None, :, None] + my_batches[:, None, :]) % reps
    match = landing[..., None] == rep_ids
    allowed = jnp.sum(jnp.where(match, counts[:, None, None, :], 0), axis=-1)
    batch_ids = section_pos * batches + jnp.arange(batches, dtype=jnp.int32)
    keep = (batch_ids < allowed).astype(F32)
    keep = jnp.transpose(keep, (1, 2, 0))
    keep = jnp.broadcast_to(keep[:, :, None, :], (reps, batches, ROWS, sections))
    keep = keep.reshape(reps * rows, sections)
    keep_own = lax.dynamic_slice_in_dim(keep, slot("rep", rep_pos, reps) * rows, rows, 0)
    x_shard, c_shard, w_all, g_all = exchange(
        [
            (x_split, "rep", True),
            (c_split, "rep", True),
            (w_pack, "section", False),
            (g_own, "section", False),
        ],
        0,
    )
    mix_width = sections // 2 * 3 * head + sections * head
    z, mixed = local_call(
        project_kernel,
        [
            jax.ShapeDtypeStruct((2, chips, rows, sections * 5 * head), BF16),
            jax.ShapeDtypeStruct((2, chips, head // reps, mix_width), BF16),
        ],
        x_shard,
        c_shard,
        w_all,
        g_all,
    )
    z, mixed = reduce_call(z, mixed, sections, 1)
    made, scal = local_call(
        functools.partial(chain_kernel, head ** (-0.5)),
        [
            jax.ShapeDtypeStruct((4, rows, sections * head), BF16),
            jax.ShapeDtypeStruct((rows, head), F32),
        ],
        x_own,
        z,
        mixed,
        keep_own,
    )
    grads = tail_call(x_shard, c_shard, made, scal, keep, w_all, g_all, 2)
    return tuple(grad[None] for grad in grads)


def on_device(*arrays):
    sections = lax.axis_size("section")
    head = arrays[2].shape[2]
    reps = lax.axis_size("rep")
    if sections == 4 and reps % 2 == 0 and head % (16 * reps) == 0:
        return low_rank(*arrays)
    return pipelined(*arrays)


def solution(mesh):
    in_specs = (
        P("rep", None),
        P("rep", None),
        P("section", "rep", None),
        P("section", "rep", None),
        P("section", "rep", None),
        P("section", "rep", None),
        P("section", None),
        P(),
        P(),
    )
    out_specs = (
        P("section", "rep", None),
        P("section", "rep", None),
        P("section", "rep", None),
        P("section", "rep", None),
    )
    return jax.shard_map(
        on_device, mesh=mesh, in_specs=in_specs, out_specs=out_specs, check_vma=False
    )
```

```python
import functools

import jax
import jax.numpy as jnp
from jax import lax
from jax.experimental import pallas as pl
from jax.experimental.pallas import tpu as pltpu
from jax.sharding import PartitionSpec as P


MB = 8
ROWS = 16


EPSILON = 1e-05


def from_behind(block, axis, distance):
    devices = range(lax.axis_size(axis))
    route = [(i - distance, i) for i in devices if i - distance in devices]
    return lax.ppermute(block, axis, route)


def attend(query, key, scale):
    rows_here = query.shape[0]
    scores = jnp.einsum("id,jd->ij", query, key, preferred_element_type=jnp.float32) * scale
    causal = jnp.arange(rows_here)[:, None] >= jnp.arange(rows_here)[None, :]
    expo = jnp.exp(jnp.where(causal, scores, -1e30))
    return expo / jnp.sum(expo, axis=-1, keepdims=True)


def forward_layer(layer_in, gain, weights, keep):
    weight_q, weight_k, weight_v, weight_o = weights
    scale = weight_q.shape[1] ** (-0.5)
    x_float = layer_in.astype(jnp.float32)
    rinv = lax.rsqrt(jnp.mean(x_float * x_float, axis=-1, keepdims=True) + EPSILON)
    normed = (x_float * rinv * gain).astype(jnp.bfloat16)
    query = jnp.dot(normed, weight_q, preferred_element_type=jnp.float32).astype(jnp.bfloat16)
    key = jnp.dot(normed, weight_k, preferred_element_type=jnp.float32).astype(jnp.bfloat16)
    value = jnp.dot(normed, weight_v, preferred_element_type=jnp.float32).astype(jnp.bfloat16)
    probs_low = attend(query, key, scale).astype(jnp.bfloat16)
    heads = jnp.dot(probs_low, value, preferred_element_type=jnp.float32).astype(jnp.bfloat16)
    output = lax.dot_general(
        heads, weight_o, (((1,), (1,)), ((), ())), preferred_element_type=jnp.float32
    )
    result = (x_float + keep * output).astype(jnp.bfloat16)
    return (result, normed, query, key, value, heads)


def backward_layer(grad_in, layer_in, query, key, value, gain, weights, keep):
    weight_q, weight_k, weight_v, weight_o = weights
    scale = weight_q.shape[1] ** (-0.5)
    grad_float = grad_in.astype(jnp.float32)
    grad_rows = (keep * grad_float).astype(jnp.bfloat16)
    d_heads = jnp.dot(grad_rows, weight_o, preferred_element_type=jnp.float32).astype(jnp.bfloat16)
    probs = attend(query, key, scale)
    probs_low = probs.astype(jnp.bfloat16)
    d_value = jnp.einsum(
        "ij,id->jd", probs_low, d_heads, preferred_element_type=jnp.float32
    ).astype(jnp.bfloat16)
    d_probs = jnp.einsum("id,jd->ij", d_heads, value, preferred_element_type=jnp.float32)
    d_score = (probs * (d_probs - jnp.sum(probs * d_probs, axis=-1, keepdims=True)) * scale).astype(
        jnp.bfloat16
    )
    d_query = jnp.dot(d_score, key, preferred_element_type=jnp.float32).astype(jnp.bfloat16)
    d_key = jnp.einsum("ij,id->jd", d_score, query, preferred_element_type=jnp.float32).astype(
        jnp.bfloat16
    )
    contract = (((1,), (1,)), ((), ()))
    d_normed = lax.dot_general(d_query, weight_q, contract, preferred_element_type=jnp.float32)
    d_normed = d_normed + lax.dot_general(
        d_key, weight_k, contract, preferred_element_type=jnp.float32
    )
    d_normed = d_normed + lax.dot_general(
        d_value, weight_v, contract, preferred_element_type=jnp.float32
    )
    x_float = layer_in.astype(jnp.float32)
    rinv = lax.rsqrt(jnp.mean(x_float * x_float, axis=-1, keepdims=True) + EPSILON)
    scaled = d_normed * gain
    d_input = rinv * (
        scaled - x_float * rinv * rinv * jnp.mean(scaled * x_float, axis=-1, keepdims=True)
    )
    return ((grad_float + d_input).astype(jnp.bfloat16), grad_rows, d_query, d_key, d_value)


def store_slot(store, value, slot_at, is_valid):
    old_value = lax.dynamic_index_in_dim(store, slot_at, 0, keepdims=False)
    fresh = jnp.where(is_valid, value, old_value)
    return lax.dynamic_update_index_in_dim(store, fresh, slot_at, 0)


def zeros_like_all(values):
    return tuple((jnp.zeros(value.shape, value.dtype) for value in values))


def pick_slot(store, slot_at):
    return lax.dynamic_index_in_dim(store, slot_at, 0, keepdims=False)


def local_grad(left, right):
    width_left = left.shape[-1]
    width_right = right.shape[-1]
    return jnp.einsum(
        "td,th->dh",
        left.reshape(-1, width_left),
        right.reshape(-1, width_right),
        preferred_element_type=jnp.float32,
    )


def pipelined(x_in, cot, w_q, w_k, w_v, w_out, gains, offsets, counts):
    section_count = lax.axis_size("section")
    rep_count = lax.axis_size("rep")
    section_pos = lax.axis_index("section")
    rep_pos = lax.axis_index("rep")
    weights = (
        lax.all_gather(w_q[0], "rep", axis=0, tiled=True),
        lax.all_gather(w_k[0], "rep", axis=0, tiled=True),
        lax.all_gather(w_v[0], "rep", axis=0, tiled=True),
        lax.all_gather(w_out[0], "rep", axis=0, tiled=True),
    )
    width = weights[0].shape[0]
    head_size = weights[0].shape[1]
    gain = gains[0]
    landing_sum = jnp.cumsum(offsets, axis=0) % rep_count
    my_offsets = lax.dynamic_index_in_dim(landing_sum, section_pos, 0, keepdims=False)
    landing = (rep_pos + my_offsets) % rep_count
    count_row = lax.dynamic_index_in_dim(counts, section_pos, 0, keepdims=False)
    match_rep = landing[:, None] == jnp.arange(rep_count, dtype=jnp.int32)[None, :]
    allowed = jnp.sum(jnp.where(match_rep, count_row[None, :], 0), axis=1)
    keeps = (jnp.arange(MB, dtype=jnp.int32) < allowed).astype(jnp.float32)
    inputs = x_in.reshape(MB, ROWS, width)
    top_grads = cot.reshape(MB, ROWS, width)
    tick_count = section_count + MB - 1
    row_block = jnp.zeros((ROWS, width), jnp.bfloat16)
    head_block = jnp.zeros((ROWS, head_size), jnp.bfloat16)

    def forward_tick(tick_no, carry):
        inbox, saved_in, saved_normed, saved_q, saved_k, saved_v, saved_heads = carry
        batch_pos = tick_no - section_pos
        is_valid = (batch_pos >= 0) & (batch_pos < MB)
        batch_at = jnp.clip(batch_pos, 0, MB - 1)
        own_rows = pick_slot(inputs, batch_at)
        layer_in = jnp.where(section_pos == 0, own_rows, inbox)
        keep = pick_slot(keeps, batch_at)
        blank = (row_block, row_block, head_block, head_block, head_block, head_block)
        made = lax.cond(
            is_valid,
            lambda rows_in: forward_layer(rows_in, gain, weights, keep),
            lambda rows_in: zeros_like_all(blank),
            layer_in,
        )
        result, normed, query, key, value, heads = made
        saved_in = store_slot(saved_in, layer_in, batch_at, is_valid)
        saved_normed = store_slot(saved_normed, normed, batch_at, is_valid)
        saved_q = store_slot(saved_q, query, batch_at, is_valid)
        saved_k = store_slot(saved_k, key, batch_at, is_valid)
        saved_v = store_slot(saved_v, value, batch_at, is_valid)
        saved_heads = store_slot(saved_heads, heads, batch_at, is_valid)
        inbox = from_behind(result, "section", 1)
        return (inbox, saved_in, saved_normed, saved_q, saved_k, saved_v, saved_heads)

    wide_store = jnp.zeros((MB, ROWS, width), jnp.bfloat16)
    head_store = jnp.zeros((MB, ROWS, head_size), jnp.bfloat16)
    start_fwd = (row_block, wide_store, wide_store, head_store, head_store, head_store, head_store)
    _, saved_in, saved_normed, saved_q, saved_k, saved_v, saved_heads = lax.fori_loop(
        0, tick_count, forward_tick, start_fwd
    )

    def backward_tick(tick_no, carry):
        inbox, saved_rows, saved_dq, saved_dk, saved_dv = carry
        batch_pos = tick_no - (section_count - 1 - section_pos)
        is_valid = (batch_pos >= 0) & (batch_pos < MB)
        batch_at = jnp.clip(batch_pos, 0, MB - 1)
        grad_in = jnp.where(section_pos == section_count - 1, pick_slot(top_grads, batch_at), inbox)
        layer_in = pick_slot(saved_in, batch_at)
        query = pick_slot(saved_q, batch_at)
        key = pick_slot(saved_k, batch_at)
        value = pick_slot(saved_v, batch_at)
        keep = pick_slot(keeps, batch_at)
        blank = (row_block, row_block, head_block, head_block, head_block)
        made = lax.cond(
            is_valid,
            lambda rows_in: backward_layer(
                rows_in, layer_in, query, key, value, gain, weights, keep
            ),
            lambda rows_in: zeros_like_all(blank),
            grad_in,
        )
        grad_back, grad_rows, d_query, d_key, d_value = made
        saved_rows = store_slot(saved_rows, grad_rows, batch_at, is_valid)
        saved_dq = store_slot(saved_dq, d_query, batch_at, is_valid)
        saved_dk = store_slot(saved_dk, d_key, batch_at, is_valid)
        saved_dv = store_slot(saved_dv, d_value, batch_at, is_valid)
        inbox = from_behind(grad_back, "section", -1)
        return (inbox, saved_rows, saved_dq, saved_dk, saved_dv)

    start_bwd = (row_block, wide_store, head_store, head_store, head_store)
    _, saved_rows, saved_dq, saved_dk, saved_dv = lax.fori_loop(
        0, tick_count, backward_tick, start_bwd
    )
    full_q = local_grad(saved_normed, saved_dq)
    full_k = local_grad(saved_normed, saved_dk)
    full_v = local_grad(saved_normed, saved_dv)
    full_o = local_grad(saved_rows, saved_heads)
    share_width = width // rep_count
    totals = (
        lax.psum(full_q.astype(jnp.bfloat16), "rep").astype(jnp.float32),
        lax.psum(full_k.astype(jnp.bfloat16), "rep").astype(jnp.float32),
        lax.psum(full_v.astype(jnp.bfloat16), "rep").astype(jnp.float32),
        lax.psum(full_o.astype(jnp.bfloat16), "rep").astype(jnp.float32),
    )
    parts = tuple(
        (lax.dynamic_slice_in_dim(total, rep_pos * share_width, share_width, 0) for total in totals)
    )
    return (parts[0][None], parts[1][None], parts[2][None], parts[3][None])


F32 = jnp.float32
BF16 = jnp.bfloat16
VMEM_LIMIT = 60 * 1024 * 1024


def vmem_specs(count):
    return [pl.BlockSpec(memory_space=pltpu.VMEM)] * count


def slot(axis, index, size):
    if axis == "rep":
        return lax.rem(index, 2) * (size // 2) + index // 2
    return index


MESH_ID = pl.DeviceIdType.MESH


def remote(src, dst, send, recv, target):
    return pltpu.make_async_remote_copy(
        src_ref=src, dst_ref=dst, send_sem=send, recv_sem=recv, device_id=target,
        device_id_type=MESH_ID,
    )


def greet(targets):
    barrier = pltpu.get_barrier_semaphore()
    for target in targets:
        pl.semaphore_signal(barrier, inc=1, device_id=target, device_id_type=MESH_ID)
    pl.semaphore_wait(barrier, len(targets))


def place(chips, sections):
    rep_pos = lax.axis_index("rep")
    core, chip = lax.rem(rep_pos, 2), rep_pos // 2
    section = lax.axis_index("section")
    partner = {"rep": chip * 2 + 1 - core}
    along = []
    for step in range(1, chips):
        to, source = lax.rem(chip + step, chips), lax.rem(chip + chips - step, chips)
        along.append((step, to, source, {"rep": to * 2 + core}))
    across = []
    for step in range(1, sections):
        to = lax.rem(section + step, sections)
        source = lax.rem(section + sections - step, sections)
        across.append((step, to, source, {"section": to}))
    return core, chip, section, partner, along, across


def dot(left, right, dims=((1,), (0,))):
    return lax.dot_general(left, right, (dims, ((), ())), preferred_element_type=F32)


def front_kernel(
    x_in, c_in, w_in, g_in,
    x_ref, c_ref, w_ref, g_ref, z_land, m_out,
    z_ref, z_core, z_sum, m_ref, m_core, m_sum, m_land, m_total,
    core_send, core_recv, z_send, z_recv, m_send, m_recv, g_send, g_recv, s_send, s_recv,
    x_send, x_recv, w_send, w_recv,
):
    sections, chips = z_land.shape[:2]
    reps, rows, shard = x_ref.shape
    head = w_ref.shape[2] // 4
    qkv = 3 * head
    half = shard // 2
    core, chip, section, partner, along, across = place(chips, sections)
    other = 1 - core
    near_x = section + 1 - 2 * lax.rem(section, 2)
    near_y = lax.rem(section + 2, 4)
    diagonal = 3 - section
    to_x, to_y = {"section": near_x}, {"section": near_y}
    me = chip * 2 + core
    peers = []
    for step in range(1, reps):
        to, source = lax.rem(me + step, reps), lax.rem(me + reps - step, reps)
        peers.append((step, to, slot("rep", source, reps), {"rep": to}))
    greet([p[3] for p in peers] + [a[3] for a in across])
    sends = []

    def start(copy):
        copy.start()
        sends.append(copy)

    first, second = pl.ds(0, half), pl.ds(half, half)

    def weight(number, src, at, rows_at, target):
        dst = w_ref.at[at, rows_at]
        return remote(src, dst, w_send.at[number], w_recv.at[number], target)

    start(weight(0, w_in.at[first], section, first, to_x))
    start(weight(1, w_in.at[second], section, second, to_y))
    for step, to, source, target in across:
        start(remote(g_in, g_ref.at[section], w_send.at[5 + step], w_recv.at[5 + step], target))
    start(weight(2, w_in.at[second], section, second, to_x))
    start(weight(3, w_in.at[first], section, first, to_y))
    mine = slot("rep", me, reps)
    for i, (src, dst) in enumerate(((x_in, x_ref), (c_in, c_ref))):
        for step, to, source, target in peers:
            start(remote(src.at[to], dst.at[mine], x_send.at[i, step], x_recv.at[i, step], target))
        dst[mine] = src[me]
    w_ref[section] = w_in[...]
    g_ref[section] = g_in[...]

    def landed(number, at, rows_at):
        ref = w_ref.at[at, rows_at]
        remote(ref, ref, w_send.at[number], w_recv.at[number], to_x).wait_recv()

    landed(0, near_x, first)
    start(weight(4, w_ref.at[near_x, first], near_x, first, to_y))
    landed(1, near_y, second)
    start(weight(5, w_ref.at[near_y, second], near_y, second, to_x))
    for step, to, source, target in across:
        at = g_ref.at[source]
        remote(at, at, w_send.at[5 + step], w_recv.at[5 + step], target).wait_recv()
    for i, dst in enumerate((x_ref, c_ref)):
        for step, to, source, target in peers:
            at = dst.at[source]
            remote(at, at, x_send.at[i, step], x_recv.at[i, step], target).wait_recv()
    x_all = x_ref[...].reshape(reps * rows, shard)
    c_all = c_ref[...].reshape(reps * rows, shard)
    wide = x_all.astype(F32)

    def put(ref, at, block):
        shape = ref.shape[:3] + (block.shape[1],)
        ref[:, :, :, at : at + block.shape[1]] = block.astype(BF16).reshape(shape)

    def chunk(i, s):
        scaled = (wide * g_ref[s]).astype(BF16)
        w_o = w_ref[s, :, qkv:]
        z = z_ref.at[i]
        put(z, 0, dot(scaled, w_ref[s, :, 0:qkv]))
        put(z, qkv, dot(x_all, w_o))
        put(z, 4 * head, dot(c_all, w_o))
        copy = remote(
            z_ref.at[i, other], z_core.at[i], core_send.at[8 + i], core_recv.at[8 + i], partner
        )
        copy.start()
        return copy

    z_copies = []

    def forward(i, s, copy):
        copy.wait()
        z_sum[i] = (z_ref[i, core].astype(F32) + z_core[i].astype(F32)).astype(BF16)
        for step, to, source, target in along:
            copy = remote(
                z_sum.at[i, to], z_land.at[s, step], z_send.at[i, step], z_recv.at[i, step], target
            )
            copy.start()
            z_copies.append(copy)
        z_land[s, 0] = z_sum[i, chip]

    forward(0, section, chunk(0, section))
    landed(2, near_x, second)
    forward(1, near_x, chunk(1, near_x))
    landed(3, near_y, first)
    landed(4, diagonal, first)
    landed(5, diagonal, second)
    for gap in range(1, sections // 2 + 1):
        far = lax.rem(section + gap, sections)
        low, high = jnp.minimum(section, far), jnp.maximum(section, far)
        turned = jnp.transpose(w_ref[low, :, qkv:].astype(F32))
        turned = (turned * g_ref[high]).astype(BF16)
        put(m_ref, (gap - 1) * qkv, dot(turned, w_ref[high, :, 0:qkv]))
    w_me = w_ref[section, :, qkv:]
    base = sections // 2 * qkv
    for s in range(sections):
        put(m_ref, base + s * head, dot(w_me, w_ref[s, :, qkv:], ((0,), (0,))))
    m_first = remote(m_ref.at[other], m_core, core_send.at[0], core_recv.at[0], partner)
    m_first.start()
    chunk_y = chunk(2, near_y)
    m_first.wait()
    m_sum[...] = (m_ref[core].astype(F32) + m_core[...].astype(F32)).astype(BF16)
    m_copies = []
    for step, to, source, target in along:
        copy = remote(m_sum.at[to], m_land.at[step], m_send.at[step], m_recv.at[step], target)
        copy.start()
        m_copies.append(copy)
    total = m_sum[chip].astype(F32)
    chunk_d = chunk(3, diagonal)
    for copy, (step, to, source, target) in zip(m_copies, along):
        copy.wait()
        total = total + m_land[step].astype(F32)
    m_total[...] = total.astype(BF16)
    spread = []
    for step, to, source, target in along:
        copy = remote(
            m_total, m_out.at[core, section, chip], g_send.at[step], g_recv.at[step], target
        )
        copy.start()
        spread.append(copy)
    m_out[core, section, chip] = total.astype(BF16)
    forward(2, near_y, chunk_y)
    forward(3, diagonal, chunk_d)
    for copy, (step, to, source, target) in zip(spread, along):
        copy.wait_send()
        at = m_out.at[core, section, source]
        remote(at, at, g_send.at[step], g_recv.at[step], target).wait_recv()
    mine = m_out.at[core, section]
    cross = []
    for step, to, source, target in across:
        copy = remote(mine, mine, s_send.at[step], s_recv.at[step], target)
        copy.start()
        cross.append(copy)
    own = remote(mine, mine, core_send.at[2], core_recv.at[2], partner)
    own.start()
    last = []
    for copy, (step, to, source, target) in zip(cross, across):
        at = m_out.at[core, source]
        remote(at, at, s_send.at[step], s_recv.at[step], target).wait_recv()
        copy = remote(at, at, core_send.at[2 + step], core_recv.at[2 + step], partner)
        copy.start()
        last.append(copy)
    for copy in z_copies:
        copy.wait()
    for copy in cross:
        copy.wait_send()
    own.wait_send()
    at = m_out.at[other, section]
    remote(at, at, core_send.at[2], core_recv.at[2], partner).wait_recv()
    for copy, (step, to, source, target) in zip(last, across):
        copy.wait_send()
        at = m_out.at[other, source]
        remote(at, at, core_send.at[2 + step], core_recv.at[2 + step], partner).wait_recv()
    for copy in sends:
        copy.wait_send()


def front_call(x, c, w, g, collective_id):
    reps, rows, shard = x.shape
    head = w.shape[1] // 4
    sections = lax.axis_size("section")
    chips = reps // 2
    block = (rows, 5 * head)
    mix = (head // reps, sections // 2 * 3 * head + sections * head)
    dma = pltpu.SemaphoreType.DMA
    return pl.pallas_call(
        front_kernel,
        out_shape=[
            jax.ShapeDtypeStruct(x.shape, BF16),
            jax.ShapeDtypeStruct(x.shape, BF16),
            jax.ShapeDtypeStruct((sections,) + w.shape, BF16),
            jax.ShapeDtypeStruct((sections,) + g.shape, F32),
            jax.ShapeDtypeStruct((sections, chips) + block, BF16),
            jax.ShapeDtypeStruct((2, sections, chips) + mix, BF16),
        ],
        in_specs=vmem_specs(4),
        out_specs=vmem_specs(6),
        scratch_shapes=[
            pltpu.VMEM((sections, 2, chips) + block, BF16),
            pltpu.VMEM((sections, chips) + block, BF16),
            pltpu.VMEM((sections, chips) + block, BF16),
            pltpu.VMEM((2, chips) + mix, BF16),
            pltpu.VMEM((chips,) + mix, BF16),
            pltpu.VMEM((chips,) + mix, BF16),
            pltpu.VMEM((chips,) + mix, BF16),
            pltpu.VMEM(mix, BF16),
            dma((12,)), dma((12,)),
            dma((sections, chips)), dma((sections, chips)), dma((chips,)), dma((chips,)),
            dma((chips,)), dma((chips,)), dma((sections,)), dma((sections,)),
            dma((2, reps)), dma((2, reps)), dma((9,)), dma((9,)),
        ],
        compiler_params=pltpu.CompilerParams(
            collective_id=collective_id, has_side_effects=True, vmem_limit_bytes=VMEM_LIMIT
        ),
    )(x, c, w, g)


def chain_kernel(scale, x_ref, z_ref, m_ref, keep_ref, out_ref, scal_ref):
    sections = keep_ref.shape[1]
    head = scal_ref.shape[1]
    rows, width = x_ref.shape
    wide = 4 * head
    x_float = x_ref[...].astype(F32)
    square = jnp.sum(x_float * x_float, axis=1, keepdims=True)
    z = [jnp.sum(z_ref[s].astype(F32), axis=0) for s in range(sections)]
    base = sections // 2 * 3 * head
    mix = [
        jnp.concatenate([m_ref[c, s].reshape(head // 2, -1) for c in range(2)], axis=0)
        for s in range(sections)
    ]

    def pair(low, high):
        gap = high - low
        owner = low
        if gap > sections // 2:
            owner, gap = high, sections - gap
        return mix[owner][:, (gap - 1) * 3 * head : gap * 3 * head]

    row = lax.broadcasted_iota(jnp.int32, (rows, rows), 0)
    col = lax.broadcasted_iota(jnp.int32, (rows, rows), 1)
    allowed = (row >= col) & (row // ROWS == col // ROWS)
    y = [z[s][:, 0 : 3 * head] for s in range(sections)]
    acto = [z[s][:, 3 * head : wide] for s in range(sections)]
    saved = []
    for s in range(sections):
        keep = keep_ref[:, s : s + 1]
        rinv = lax.rsqrt(jnp.maximum(square, 0.0) / width + EPSILON)
        qkv = (y[s] * rinv).astype(BF16)
        query, key, value = qkv[:, 0:head], qkv[:, head : 2 * head], qkv[:, 2 * head :]
        scores = dot(query, key, ((1,), (1,))) * scale
        expo = jnp.exp(jnp.where(allowed, scores, -1e30))
        probs = expo / jnp.sum(expo, axis=1, keepdims=True)
        low = probs.astype(BF16)
        heads = dot(low, value).astype(BF16)
        kept = heads.astype(F32) * keep
        kept_low = kept.astype(BF16)
        saved.append((rinv, query, key, value, probs, low, acto[:], y[s]))
        out_ref[0, :, s * head : (s + 1) * head] = heads
        moved = dot(kept_low, mix[s][:, base:])
        square = square + jnp.sum(
            kept * (2.0 * acto[s] + moved[:, s * head : (s + 1) * head]),
            axis=1,
            keepdims=True,
        )
        for t in range(sections):
            if t > s:
                y[t] = y[t] + dot(kept_low, pair(s, t))
            acto[t] = acto[t] + moved[:, t * head : (t + 1) * head]
    bo = [z[s][:, wide:] for s in range(sections)]
    lane = lax.broadcasted_iota(jnp.int32, (rows, head), 1)
    scal = jnp.zeros((rows, head), F32)
    for s in range(sections - 1, -1, -1):
        keep = keep_ref[:, s : s + 1]
        rinv, query, key, value, probs, low, act_o, y_s = saved[s]
        d_heads = (keep * bo[s]).astype(BF16)
        d_value = dot(low, d_heads, ((0,), (0,))).astype(BF16)
        d_probs = dot(d_heads, value, ((1,), (1,)))
        d_score = (
            probs * (d_probs - jnp.sum(probs * d_probs, axis=1, keepdims=True)) * scale
        ).astype(BF16)
        d_query = dot(d_score, key).astype(BF16)
        d_key = dot(d_score, query, ((0,), (0,))).astype(BF16)
        grads = jnp.concatenate([d_query, d_key, d_value], axis=1)
        out_ref[1, :, s * head : (s + 1) * head] = d_value
        out_ref[2, :, s * head : (s + 1) * head] = d_query
        out_ref[3, :, s * head : (s + 1) * head] = d_key
        mean = jnp.sum(grads.astype(F32) * y_s, axis=1, keepdims=True) / width
        pull = rinv * rinv * rinv * mean
        scal = jnp.where(lane == s, rinv, scal)
        scal = jnp.where(lane == sections + s, pull, scal)
        for t in range(s):
            part = dot(grads, pair(t, s), ((1,), (1,)))
            bo[t] = bo[t] + rinv * part - pull * act_o[t]
    scal_ref[...] = scal


def tail_kernel(
    x_ref, c_ref, made_ref, scal_ref, keep_ref, w_ref, g_ref,
    out_ref,
    made, scal, normed, acts, part, relay, from_x, from_y, merged,
    z_send, z_recv, core_send, core_recv, h_send, h_recv,
):
    reps, rows, shard = x_ref.shape
    sections = w_ref.shape[0]
    head = w_ref.shape[2] // 4
    qkv = 3 * head
    half = shard // 2
    chips = reps // 2
    total = reps * rows
    core, chip, section, partner, along, _ = place(chips, 1)
    other = 1 - core
    near_x = section + 1 - 2 * lax.rem(section, 2)
    near_y = lax.rem(section + 2, 4)
    diagonal = 3 - section
    to_x, to_y = {"section": near_x}, {"section": near_y}
    greet([partner] + [a[3] for a in along] + [to_x, to_y])
    outs = [made.at[i] for i in range(4)] + [scal]
    ins = [made_ref.at[i] for i in range(4)] + [scal_ref]
    sends = []

    def start(copy):
        copy.start()
        sends.append(copy)

    for i in (4, 0, 1, 2, 3):
        for step, to, source, target in along:
            at = outs[i].at[core, chip]
            start(remote(ins[i], at, z_send.at[i, step], z_recv.at[i, step], target))
        at = outs[i].at[core, chip]
        start(remote(ins[i], at, core_send.at[i, 0], core_recv.at[i, 0], partner))
    for i in range(4):
        made[i, core, chip] = made_ref[i]
    scal[core, chip] = scal_ref[...]

    def arrive(kinds):
        for i in kinds:
            for step, to, source, target in along:
                at = outs[i].at[core, source]
                remote(at, at, z_send.at[i, step], z_recv.at[i, step], target).wait_recv()
                start(remote(at, at, core_send.at[i, step], core_recv.at[i, step], partner))
        for i in kinds:
            for step, source in [(0, chip)] + [(a[0], a[2]) for a in along]:
                at = outs[i].at[other, source]
                remote(at, at, core_send.at[i, step], core_recv.at[i, step], partner).wait_recv()

    first, second = pl.ds(0, half), pl.ds(half, half)

    def message(kind, number, src, dst, target):
        return remote(src, dst, h_send.at[kind, number], h_recv.at[kind, number], target)

    def messages(kind):
        p = part.at[kind]
        return [
            message(kind, 0, p.at[diagonal, first], relay.at[kind, 0], to_x),
            message(kind, 1, p.at[near_x, first], from_x.at[kind, first], to_x),
            message(kind, 2, merged.at[kind, 1], from_x.at[kind, second], to_x),
            message(kind, 3, p.at[diagonal, second], relay.at[kind, 1], to_y),
            message(kind, 4, p.at[near_y, second], from_y.at[kind, second], to_y),
            message(kind, 5, merged.at[kind, 0], from_y.at[kind, first], to_y),
        ]

    def send_parts(kind):
        copies = messages(kind)
        for number in (0, 3, 1, 4):
            start(copies[number])

    def send_merged(kind):
        copies = messages(kind)
        copies[0].wait_recv()
        merged[kind, 0] = (
            relay[kind, 0].astype(F32) + part[kind, near_y, 0:half].astype(F32)
        ).astype(BF16)
        start(copies[5])
        copies[3].wait_recv()
        merged[kind, 1] = (
            relay[kind, 1].astype(F32) + part[kind, near_x, half:].astype(F32)
        ).astype(BF16)
        start(copies[2])

    def block(kind, s):
        return made[kind, :, :, :, s * head : (s + 1) * head].reshape(total, head)

    def column(at):
        return scal[:, :, :, at : at + 1].reshape(total, 1)

    over = ((0,), (0,))
    across = ((1,), (1,))
    arrive((4, 0, 1))
    act = x_ref[...].reshape(total, shard).astype(F32)
    for s in range(sections):
        acts[s] = act.astype(BF16)
        normed[s] = (act * column(s) * g_ref[s]).astype(BF16)
        part[2, s] = dot(normed[s], block(1, s), over).astype(BF16)
        if s + 1 < sections:
            push = dot(block(0, s), w_ref[s, :, qkv:], across)
            act = (act + keep_ref[:, s : s + 1] * push).astype(BF16).astype(F32)
    send_parts(2)
    arrive((2,))
    for s in range(sections):
        part[0, s] = dot(normed[s], block(2, s), over).astype(BF16)
    send_parts(0)
    arrive((3,))
    for s in range(sections):
        part[1, s] = dot(normed[s], block(3, s), over).astype(BF16)
    send_merged(2)
    send_parts(1)
    back = c_ref[...].reshape(total, shard).astype(F32)
    for s in range(sections - 1, -1, -1):
        grad_rows = (keep_ref[:, s : s + 1] * back).astype(BF16)
        part[3, s] = dot(grad_rows, block(0, s), over).astype(BF16)
        if s > 0:
            d_normed = dot(block(2, s), w_ref[s, :, 0:head], across)
            d_normed = d_normed + dot(block(3, s), w_ref[s, :, head : 2 * head], across)
            d_normed = d_normed + dot(block(1, s), w_ref[s, :, 2 * head : qkv], across)
            pull = column(sections + s)
            back = back + column(s) * (d_normed * g_ref[s]) - pull * acts[s].astype(F32)
            back = back.astype(BF16).astype(F32)
    send_merged(0)
    send_parts(3)
    send_merged(1)

    def finish(kind):
        copies = messages(kind)
        for number in (1, 2, 4, 5):
            copies[number].wait_recv()
        out_ref[kind] = (
            part[kind, section].astype(F32)
            + from_x[kind].astype(F32)
            + from_y[kind].astype(F32)
        )

    finish(2)
    send_merged(3)
    finish(0)
    finish(1)
    finish(3)
    for copy in sends:
        copy.wait_send()


def tail_call(x, c, made, scal, keep, w, g, collective_id):
    reps, rows, shard = x.shape
    sections = w.shape[0]
    head = w.shape[2] // 4
    total, half = reps * rows, shard // 2
    chips = reps // 2
    dma = pltpu.SemaphoreType.DMA
    return pl.pallas_call(
        tail_kernel,
        out_shape=[jax.ShapeDtypeStruct((4, shard, head), F32)],
        in_specs=vmem_specs(7),
        out_specs=vmem_specs(1),
        scratch_shapes=[
            pltpu.VMEM((4, 2, chips) + made.shape[1:], BF16),
            pltpu.VMEM((2, chips) + scal.shape, F32),
            pltpu.VMEM((sections, total, shard), BF16),
            pltpu.VMEM((sections, total, shard), BF16),
            pltpu.VMEM((4, sections, shard, head), BF16),
            pltpu.VMEM((4, 2, half, head), BF16),
            pltpu.VMEM((4, shard, head), BF16),
            pltpu.VMEM((4, shard, head), BF16),
            pltpu.VMEM((4, 2, half, head), BF16),
            dma((5, chips)), dma((5, chips)), dma((5, chips)), dma((5, chips)),
            dma((4, 6)), dma((4, 6)),
        ],
        compiler_params=pltpu.CompilerParams(
            collective_id=collective_id, has_side_effects=True, vmem_limit_bytes=VMEM_LIMIT
        ),
    )(x, c, made, scal, keep, w, g)


def local_call(kernel, shapes, *arrays):
    return pl.pallas_call(
        kernel,
        out_shape=shapes,
        in_specs=vmem_specs(len(arrays)),
        out_specs=vmem_specs(len(shapes)),
        compiler_params=pltpu.CompilerParams(vmem_limit_bytes=VMEM_LIMIT),
    )(*arrays)


def low_rank(x_in, cot, w_q, w_k, w_v, w_out, gains, offsets, counts):
    sections = lax.axis_size("section")
    reps = lax.axis_size("rep")
    section_pos = lax.axis_index("section")
    rep_pos = lax.axis_index("rep")
    width = x_in.shape[1]
    shard, head = w_q.shape[1:]
    batches = MB // sections
    chips = reps // 2
    rows = batches * ROWS
    wide = 4 * head
    x_own = lax.dynamic_slice_in_dim(x_in, section_pos * rows, rows, 0)
    c_own = lax.dynamic_slice_in_dim(cot, section_pos * rows, rows, 0)
    x_split = x_own.reshape(rows, reps, shard).swapaxes(0, 1)
    c_split = c_own.reshape(rows, reps, shard).swapaxes(0, 1)
    w_pack = jnp.concatenate([w_q[0], w_k[0], w_v[0], w_out[0]], axis=1)
    g_own = lax.dynamic_slice_in_dim(gains, rep_pos * shard, shard, 1)
    running = jnp.zeros_like(offsets[0])
    landed = []
    for s in range(sections):
        running = running + offsets[s]
        landed.append(running % reps)
    landed = jnp.stack(landed)
    my_batches = lax.dynamic_slice_in_dim(landed, section_pos * batches, batches, 1)
    rep_ids = jnp.arange(reps, dtype=jnp.int32)
    slots = (rep_ids % chips) * 2 + rep_ids // chips
    landing = (slots[None, :, None] + my_batches[:, None, :]) % reps
    match = landing[..., None] == rep_ids
    allowed = jnp.sum(jnp.where(match, counts[:, None, None, :], 0), axis=-1)
    batch_ids = section_pos * batches + jnp.arange(batches, dtype=jnp.int32)
    keep = (batch_ids < allowed).astype(F32)
    keep = jnp.transpose(keep, (1, 2, 0))
    keep = jnp.broadcast_to(keep[:, :, None, :], (reps, batches, ROWS, sections))
    keep = keep.reshape(reps * rows, sections)
    keep_own = lax.dynamic_slice_in_dim(keep, slot("rep", rep_pos, reps) * rows, rows, 0)
    x_shard, c_shard, w_all, g_all, z, mixed = front_call(x_split, c_split, w_pack, g_own, 0)
    made, scal = local_call(
        functools.partial(chain_kernel, head ** (-0.5)),
        [
            jax.ShapeDtypeStruct((4, rows, sections * head), BF16),
            jax.ShapeDtypeStruct((rows, head), F32),
        ],
        x_own,
        z,
        mixed,
        keep_own,
    )
    (grads,) = tail_call(x_shard, c_shard, made, scal, keep, w_all, g_all, 2)
    return tuple(grads[i][None] for i in range(4))


def on_device(*arrays):
    sections = lax.axis_size("section")
    head = arrays[2].shape[2]
    reps = lax.axis_size("rep")
    if sections == 4 and reps % 2 == 0 and head % (16 * reps) == 0:
        return low_rank(*arrays)
    return pipelined(*arrays)


def solution(mesh):
    in_specs = (
        P("rep", None),
        P("rep", None),
        P("section", "rep", None),
        P("section", "rep", None),
        P("section", "rep", None),
        P("section", "rep", None),
        P("section", None),
        P(),
        P(),
    )
    out_specs = (
        P("section", "rep", None),
        P("section", "rep", None),
        P("section", "rep", None),
        P("section", "rep", None),
    )
    return jax.shard_map(
        on_device, mesh=mesh, in_specs=in_specs, out_specs=out_specs, check_vma=False
    )
```

```python
import functools

import jax
import jax.numpy as jnp
from jax import lax
from jax.experimental import pallas as pl
from jax.experimental.pallas import tpu as pltpu
from jax.sharding import PartitionSpec as P


MB = 8
ROWS = 16


EPSILON = 1e-05


def from_behind(block, axis, distance):
    devices = range(lax.axis_size(axis))
    route = [(i - distance, i) for i in devices if i - distance in devices]
    return lax.ppermute(block, axis, route)


def attend(query, key, scale):
    rows_here = query.shape[0]
    scores = jnp.einsum("id,jd->ij", query, key, preferred_element_type=jnp.float32) * scale
    causal = jnp.arange(rows_here)[:, None] >= jnp.arange(rows_here)[None, :]
    expo = jnp.exp(jnp.where(causal, scores, -1e30))
    return expo / jnp.sum(expo, axis=-1, keepdims=True)


def forward_layer(layer_in, gain, weights, keep):
    weight_q, weight_k, weight_v, weight_o = weights
    scale = weight_q.shape[1] ** (-0.5)
    x_float = layer_in.astype(jnp.float32)
    rinv = lax.rsqrt(jnp.mean(x_float * x_float, axis=-1, keepdims=True) + EPSILON)
    normed = (x_float * rinv * gain).astype(jnp.bfloat16)
    query = jnp.dot(normed, weight_q, preferred_element_type=jnp.float32).astype(jnp.bfloat16)
    key = jnp.dot(normed, weight_k, preferred_element_type=jnp.float32).astype(jnp.bfloat16)
    value = jnp.dot(normed, weight_v, preferred_element_type=jnp.float32).astype(jnp.bfloat16)
    probs_low = attend(query, key, scale).astype(jnp.bfloat16)
    heads = jnp.dot(probs_low, value, preferred_element_type=jnp.float32).astype(jnp.bfloat16)
    output = lax.dot_general(
        heads, weight_o, (((1,), (1,)), ((), ())), preferred_element_type=jnp.float32
    )
    result = (x_float + keep * output).astype(jnp.bfloat16)
    return (result, normed, query, key, value, heads)


def backward_layer(grad_in, layer_in, query, key, value, gain, weights, keep):
    weight_q, weight_k, weight_v, weight_o = weights
    scale = weight_q.shape[1] ** (-0.5)
    grad_float = grad_in.astype(jnp.float32)
    grad_rows = (keep * grad_float).astype(jnp.bfloat16)
    d_heads = jnp.dot(grad_rows, weight_o, preferred_element_type=jnp.float32).astype(jnp.bfloat16)
    probs = attend(query, key, scale)
    probs_low = probs.astype(jnp.bfloat16)
    d_value = jnp.einsum(
        "ij,id->jd", probs_low, d_heads, preferred_element_type=jnp.float32
    ).astype(jnp.bfloat16)
    d_probs = jnp.einsum("id,jd->ij", d_heads, value, preferred_element_type=jnp.float32)
    d_score = (probs * (d_probs - jnp.sum(probs * d_probs, axis=-1, keepdims=True)) * scale).astype(
        jnp.bfloat16
    )
    d_query = jnp.dot(d_score, key, preferred_element_type=jnp.float32).astype(jnp.bfloat16)
    d_key = jnp.einsum("ij,id->jd", d_score, query, preferred_element_type=jnp.float32).astype(
        jnp.bfloat16
    )
    contract = (((1,), (1,)), ((), ()))
    d_normed = lax.dot_general(d_query, weight_q, contract, preferred_element_type=jnp.float32)
    d_normed = d_normed + lax.dot_general(
        d_key, weight_k, contract, preferred_element_type=jnp.float32
    )
    d_normed = d_normed + lax.dot_general(
        d_value, weight_v, contract, preferred_element_type=jnp.float32
    )
    x_float = layer_in.astype(jnp.float32)
    rinv = lax.rsqrt(jnp.mean(x_float * x_float, axis=-1, keepdims=True) + EPSILON)
    scaled = d_normed * gain
    d_input = rinv * (
        scaled - x_float * rinv * rinv * jnp.mean(scaled * x_float, axis=-1, keepdims=True)
    )
    return ((grad_float + d_input).astype(jnp.bfloat16), grad_rows, d_query, d_key, d_value)


def store_slot(store, value, slot_at, is_valid):
    old_value = lax.dynamic_index_in_dim(store, slot_at, 0, keepdims=False)
    fresh = jnp.where(is_valid, value, old_value)
    return lax.dynamic_update_index_in_dim(store, fresh, slot_at, 0)


def zeros_like_all(values):
    return tuple((jnp.zeros(value.shape, value.dtype) for value in values))


def pick_slot(store, slot_at):
    return lax.dynamic_index_in_dim(store, slot_at, 0, keepdims=False)


def local_grad(left, right):
    width_left = left.shape[-1]
    width_right = right.shape[-1]
    return jnp.einsum(
        "td,th->dh",
        left.reshape(-1, width_left),
        right.reshape(-1, width_right),
        preferred_element_type=jnp.float32,
    )


def pipelined(x_in, cot, w_q, w_k, w_v, w_out, gains, offsets, counts):
    section_count = lax.axis_size("section")
    rep_count = lax.axis_size("rep")
    section_pos = lax.axis_index("section")
    rep_pos = lax.axis_index("rep")
    weights = (
        lax.all_gather(w_q[0], "rep", axis=0, tiled=True),
        lax.all_gather(w_k[0], "rep", axis=0, tiled=True),
        lax.all_gather(w_v[0], "rep", axis=0, tiled=True),
        lax.all_gather(w_out[0], "rep", axis=0, tiled=True),
    )
    width = weights[0].shape[0]
    head_size = weights[0].shape[1]
    gain = gains[0]
    landing_sum = jnp.cumsum(offsets, axis=0) % rep_count
    my_offsets = lax.dynamic_index_in_dim(landing_sum, section_pos, 0, keepdims=False)
    landing = (rep_pos + my_offsets) % rep_count
    count_row = lax.dynamic_index_in_dim(counts, section_pos, 0, keepdims=False)
    match_rep = landing[:, None] == jnp.arange(rep_count, dtype=jnp.int32)[None, :]
    allowed = jnp.sum(jnp.where(match_rep, count_row[None, :], 0), axis=1)
    keeps = (jnp.arange(MB, dtype=jnp.int32) < allowed).astype(jnp.float32)
    inputs = x_in.reshape(MB, ROWS, width)
    top_grads = cot.reshape(MB, ROWS, width)
    tick_count = section_count + MB - 1
    row_block = jnp.zeros((ROWS, width), jnp.bfloat16)
    head_block = jnp.zeros((ROWS, head_size), jnp.bfloat16)

    def forward_tick(tick_no, carry):
        inbox, saved_in, saved_normed, saved_q, saved_k, saved_v, saved_heads = carry
        batch_pos = tick_no - section_pos
        is_valid = (batch_pos >= 0) & (batch_pos < MB)
        batch_at = jnp.clip(batch_pos, 0, MB - 1)
        own_rows = pick_slot(inputs, batch_at)
        layer_in = jnp.where(section_pos == 0, own_rows, inbox)
        keep = pick_slot(keeps, batch_at)
        blank = (row_block, row_block, head_block, head_block, head_block, head_block)
        made = lax.cond(
            is_valid,
            lambda rows_in: forward_layer(rows_in, gain, weights, keep),
            lambda rows_in: zeros_like_all(blank),
            layer_in,
        )
        result, normed, query, key, value, heads = made
        saved_in = store_slot(saved_in, layer_in, batch_at, is_valid)
        saved_normed = store_slot(saved_normed, normed, batch_at, is_valid)
        saved_q = store_slot(saved_q, query, batch_at, is_valid)
        saved_k = store_slot(saved_k, key, batch_at, is_valid)
        saved_v = store_slot(saved_v, value, batch_at, is_valid)
        saved_heads = store_slot(saved_heads, heads, batch_at, is_valid)
        inbox = from_behind(result, "section", 1)
        return (inbox, saved_in, saved_normed, saved_q, saved_k, saved_v, saved_heads)

    wide_store = jnp.zeros((MB, ROWS, width), jnp.bfloat16)
    head_store = jnp.zeros((MB, ROWS, head_size), jnp.bfloat16)
    start_fwd = (row_block, wide_store, wide_store, head_store, head_store, head_store, head_store)
    _, saved_in, saved_normed, saved_q, saved_k, saved_v, saved_heads = lax.fori_loop(
        0, tick_count, forward_tick, start_fwd
    )

    def backward_tick(tick_no, carry):
        inbox, saved_rows, saved_dq, saved_dk, saved_dv = carry
        batch_pos = tick_no - (section_count - 1 - section_pos)
        is_valid = (batch_pos >= 0) & (batch_pos < MB)
        batch_at = jnp.clip(batch_pos, 0, MB - 1)
        grad_in = jnp.where(section_pos == section_count - 1, pick_slot(top_grads, batch_at), inbox)
        layer_in = pick_slot(saved_in, batch_at)
        query = pick_slot(saved_q, batch_at)
        key = pick_slot(saved_k, batch_at)
        value = pick_slot(saved_v, batch_at)
        keep = pick_slot(keeps, batch_at)
        blank = (row_block, row_block, head_block, head_block, head_block)
        made = lax.cond(
            is_valid,
            lambda rows_in: backward_layer(
                rows_in, layer_in, query, key, value, gain, weights, keep
            ),
            lambda rows_in: zeros_like_all(blank),
            grad_in,
        )
        grad_back, grad_rows, d_query, d_key, d_value = made
        saved_rows = store_slot(saved_rows, grad_rows, batch_at, is_valid)
        saved_dq = store_slot(saved_dq, d_query, batch_at, is_valid)
        saved_dk = store_slot(saved_dk, d_key, batch_at, is_valid)
        saved_dv = store_slot(saved_dv, d_value, batch_at, is_valid)
        inbox = from_behind(grad_back, "section", -1)
        return (inbox, saved_rows, saved_dq, saved_dk, saved_dv)

    start_bwd = (row_block, wide_store, head_store, head_store, head_store)
    _, saved_rows, saved_dq, saved_dk, saved_dv = lax.fori_loop(
        0, tick_count, backward_tick, start_bwd
    )
    full_q = local_grad(saved_normed, saved_dq)
    full_k = local_grad(saved_normed, saved_dk)
    full_v = local_grad(saved_normed, saved_dv)
    full_o = local_grad(saved_rows, saved_heads)
    share_width = width // rep_count
    totals = (
        lax.psum(full_q.astype(jnp.bfloat16), "rep").astype(jnp.float32),
        lax.psum(full_k.astype(jnp.bfloat16), "rep").astype(jnp.float32),
        lax.psum(full_v.astype(jnp.bfloat16), "rep").astype(jnp.float32),
        lax.psum(full_o.astype(jnp.bfloat16), "rep").astype(jnp.float32),
    )
    parts = tuple(
        (lax.dynamic_slice_in_dim(total, rep_pos * share_width, share_width, 0) for total in totals)
    )
    return (parts[0][None], parts[1][None], parts[2][None], parts[3][None])


F32 = jnp.float32
BF16 = jnp.bfloat16
VMEM_LIMIT = 60 * 1024 * 1024


def vmem_specs(count):
    return [pl.BlockSpec(memory_space=pltpu.VMEM)] * count


def slot(axis, index, size):
    if axis == "rep":
        return lax.rem(index, 2) * (size // 2) + index // 2
    return index


MESH_ID = pl.DeviceIdType.MESH


def remote(src, dst, send, recv, target):
    return pltpu.make_async_remote_copy(
        src_ref=src, dst_ref=dst, send_sem=send, recv_sem=recv, device_id=target,
        device_id_type=MESH_ID,
    )


def greet(targets):
    barrier = pltpu.get_barrier_semaphore()
    for target in targets:
        pl.semaphore_signal(barrier, inc=1, device_id=target, device_id_type=MESH_ID)
    pl.semaphore_wait(barrier, len(targets))


def place(chips, sections):
    rep_pos = lax.axis_index("rep")
    core, chip = lax.rem(rep_pos, 2), rep_pos // 2
    section = lax.axis_index("section")
    partner = {"rep": chip * 2 + 1 - core}
    along = []
    for step in range(1, chips):
        to, source = lax.rem(chip + step, chips), lax.rem(chip + chips - step, chips)
        along.append((step, to, source, {"rep": to * 2 + core}))
    across = []
    for step in range(1, sections):
        to = lax.rem(section + step, sections)
        source = lax.rem(section + sections - step, sections)
        across.append((step, to, source, {"section": to}))
    return core, chip, section, partner, along, across


def dot(left, right, dims=((1,), (0,))):
    return lax.dot_general(left, right, (dims, ((), ())), preferred_element_type=F32)


def front_kernel(
    x_in, c_in, w_in, g_in,
    x_ref, c_ref, w_ref, g_ref, z_land, m_out,
    z_ref, z_core, z_sum, z_mid, z_far, m_ref, m_core, m_sum, m_land, m_total,
    core_send, core_recv, z_send, z_recv, m_send, m_recv, g_send, g_recv, s_send, s_recv,
    x_send, x_recv, w_send, w_recv,
):
    sections = z_land.shape[0]
    reps, rows, shard = x_ref.shape
    chips = reps // 2
    head = w_ref.shape[2] // 4
    qkv = 3 * head
    half = shard // 2
    core, chip, section, partner, along, across = place(chips, sections)
    other = 1 - core
    near_x = section + 1 - 2 * lax.rem(section, 2)
    near_y = lax.rem(section + 2, 4)
    diagonal = 3 - section
    to_x, to_y = {"section": near_x}, {"section": near_y}
    me = chip * 2 + core
    peers = []
    for step in range(1, reps):
        to, source = lax.rem(me + step, reps), lax.rem(me + reps - step, reps)
        peers.append((step, to, slot("rep", source, reps), {"rep": to}))
    greet([p[3] for p in peers] + [a[3] for a in across])
    sends = []

    def start(copy):
        copy.start()
        sends.append(copy)

    first, second = pl.ds(0, half), pl.ds(half, half)

    def weight(number, src, at, rows_at, target):
        dst = w_ref.at[at, rows_at]
        return remote(src, dst, w_send.at[number], w_recv.at[number], target)

    start(weight(0, w_in.at[first], section, first, to_x))
    start(weight(1, w_in.at[second], section, second, to_y))
    for step, to, source, target in across:
        start(remote(g_in, g_ref.at[section], w_send.at[5 + step], w_recv.at[5 + step], target))
    start(weight(2, w_in.at[second], section, second, to_x))
    start(weight(3, w_in.at[first], section, first, to_y))
    mine = slot("rep", me, reps)
    own_rows = pl.ds(pl.multiple_of(section * rows, rows), rows)
    for i, (src, dst) in enumerate(((x_in, x_ref), (c_in, c_ref))):
        for step, to, source, target in peers:
            at = src.at[own_rows, pl.ds(pl.multiple_of(to * shard, shard), shard)]
            start(remote(at, dst.at[mine], x_send.at[i, step], x_recv.at[i, step], target))
        dst[mine] = src[own_rows, pl.ds(pl.multiple_of(me * shard, shard), shard)]
    w_ref[section] = w_in[...]
    g_ref[section] = g_in[...]

    def landed(number, at, rows_at):
        ref = w_ref.at[at, rows_at]
        remote(ref, ref, w_send.at[number], w_recv.at[number], to_x).wait_recv()

    landed(0, near_x, first)
    start(weight(4, w_ref.at[near_x, first], near_x, first, to_y))
    landed(1, near_y, second)
    start(weight(5, w_ref.at[near_y, second], near_y, second, to_x))
    for step, to, source, target in across:
        at = g_ref.at[source]
        remote(at, at, w_send.at[5 + step], w_recv.at[5 + step], target).wait_recv()
    for i, dst in enumerate((x_ref, c_ref)):
        for step, to, source, target in peers:
            at = dst.at[source]
            remote(at, at, x_send.at[i, step], x_recv.at[i, step], target).wait_recv()
    x_all = x_ref[...].reshape(reps * rows, shard)
    c_all = c_ref[...].reshape(reps * rows, shard)
    wide = x_all.astype(F32)

    def put(ref, at, block):
        shape = ref.shape[:3] + (block.shape[1],)
        ref[:, :, :, at : at + block.shape[1]] = block.astype(BF16).reshape(shape)

    def chunk(i, s):
        scaled = (wide * g_ref[s]).astype(BF16)
        w_o = w_ref[s, :, qkv:]
        z = z_ref.at[i]
        put(z, 0, dot(scaled, w_ref[s, :, 0:qkv]))
        put(z, qkv, dot(x_all, w_o))
        put(z, 4 * head, dot(c_all, w_o))
        copy = remote(
            z_ref.at[i, other], z_core.at[i], core_send.at[8 + i], core_recv.at[8 + i], partner
        )
        copy.start()
        return copy

    z_copies, halves = [], []
    beside = chip + 1 - 2 * lax.rem(chip, 2)
    away = lax.rem(chip + 2, 4)
    to_beside, to_away = {"rep": beside * 2 + core}, {"rep": away * 2 + core}

    def forward(i, s, copy):
        copy.wait()
        z_sum[i] = (z_ref[i, core].astype(F32) + z_core[i].astype(F32)).astype(BF16)
        for j, to in ((1, lax.rem(beside + 2, 4)), (0, beside)):
            copy = remote(
                z_sum.at[i, to], z_mid.at[i, j], z_send.at[i, j], z_recv.at[i, j], to_beside
            )
            copy.start()
            halves.append((i, j, copy))

    def second_hop(i, s):
        for at, j, copy in halves:
            if at == i:
                copy.wait()
        z_far[i] = (z_sum[i, away].astype(F32) + z_mid[i, 1].astype(F32)).astype(BF16)
        copy = remote(z_far.at[i], z_land.at[s, 1], z_send.at[i, 2], z_recv.at[i, 2], to_away)
        copy.start()
        z_copies.append(copy)
        z_land[s, 0] = (z_sum[i, chip].astype(F32) + z_mid[i, 0].astype(F32)).astype(BF16)

    forward(0, section, chunk(0, section))
    landed(2, near_x, second)
    chunk_x = chunk(1, near_x)
    second_hop(0, section)
    forward(1, near_x, chunk_x)
    landed(3, near_y, first)
    landed(4, diagonal, first)
    landed(5, diagonal, second)
    for gap in range(1, sections // 2 + 1):
        far = lax.rem(section + gap, sections)
        low, high = jnp.minimum(section, far), jnp.maximum(section, far)
        turned = jnp.transpose(w_ref[low, :, qkv:].astype(F32))
        turned = (turned * g_ref[high]).astype(BF16)
        put(m_ref, (gap - 1) * qkv, dot(turned, w_ref[high, :, 0:qkv]))
    w_me = w_ref[section, :, qkv:]
    base = sections // 2 * qkv
    for s in range(sections):
        put(m_ref, base + s * head, dot(w_me, w_ref[s, :, qkv:], ((0,), (0,))))
    m_first = remote(m_ref.at[other], m_core, core_send.at[0], core_recv.at[0], partner)
    m_first.start()
    chunk_y = chunk(2, near_y)
    m_first.wait()
    m_sum[...] = (m_ref[core].astype(F32) + m_core[...].astype(F32)).astype(BF16)
    m_copies = []
    for step, to, source, target in along:
        copy = remote(m_sum.at[to], m_land.at[step], m_send.at[step], m_recv.at[step], target)
        copy.start()
        m_copies.append(copy)
    total = m_sum[chip].astype(F32)
    chunk_d = chunk(3, diagonal)
    second_hop(1, near_x)
    for copy, (step, to, source, target) in zip(m_copies, along):
        copy.wait()
        total = total + m_land[step].astype(F32)
    m_total[...] = total.astype(BF16)
    spread = []
    for step, to, source, target in along:
        copy = remote(
            m_total, m_out.at[core, section, chip], g_send.at[step], g_recv.at[step], target
        )
        copy.start()
        spread.append(copy)
    m_out[core, section, chip] = total.astype(BF16)
    forward(2, near_y, chunk_y)
    forward(3, diagonal, chunk_d)
    for copy, (step, to, source, target) in zip(spread, along):
        copy.wait_send()
        at = m_out.at[core, section, source]
        remote(at, at, g_send.at[step], g_recv.at[step], target).wait_recv()
    mine = m_out.at[core, section]
    cross = []
    for step, to, source, target in across:
        copy = remote(mine, mine, s_send.at[step], s_recv.at[step], target)
        copy.start()
        cross.append(copy)
    own = remote(mine, mine, core_send.at[2], core_recv.at[2], partner)
    own.start()
    second_hop(2, near_y)
    second_hop(3, diagonal)
    last = []
    for copy, (step, to, source, target) in zip(cross, across):
        at = m_out.at[core, source]
        remote(at, at, s_send.at[step], s_recv.at[step], target).wait_recv()
        copy = remote(at, at, core_send.at[2 + step], core_recv.at[2 + step], partner)
        copy.start()
        last.append(copy)
    for copy in z_copies:
        copy.wait()
    for copy in cross:
        copy.wait_send()
    own.wait_send()
    at = m_out.at[other, section]
    remote(at, at, core_send.at[2], core_recv.at[2], partner).wait_recv()
    for copy, (step, to, source, target) in zip(last, across):
        copy.wait_send()
        at = m_out.at[other, source]
        remote(at, at, core_send.at[2 + step], core_recv.at[2 + step], partner).wait_recv()
    for copy in sends:
        copy.wait_send()


def front_call(x, c, w, g, rows, collective_id):
    shard = w.shape[0]
    reps = x.shape[1] // shard
    head = w.shape[1] // 4
    sections = lax.axis_size("section")
    chips = reps // 2
    block = (rows, 5 * head)
    mix = (head // reps, sections // 2 * 3 * head + sections * head)
    dma = pltpu.SemaphoreType.DMA
    return pl.pallas_call(
        front_kernel,
        out_shape=[
            jax.ShapeDtypeStruct((reps, rows, shard), BF16),
            jax.ShapeDtypeStruct((reps, rows, shard), BF16),
            jax.ShapeDtypeStruct((sections,) + w.shape, BF16),
            jax.ShapeDtypeStruct((sections,) + g.shape, F32),
            jax.ShapeDtypeStruct((sections, 2) + block, BF16),
            jax.ShapeDtypeStruct((2, sections, chips) + mix, BF16),
        ],
        in_specs=vmem_specs(4),
        out_specs=vmem_specs(6),
        scratch_shapes=[
            pltpu.VMEM((sections, 2, chips) + block, BF16),
            pltpu.VMEM((sections, chips) + block, BF16),
            pltpu.VMEM((sections, chips) + block, BF16),
            pltpu.VMEM((sections, 2) + block, BF16),
            pltpu.VMEM((sections,) + block, BF16),
            pltpu.VMEM((2, chips) + mix, BF16),
            pltpu.VMEM((chips,) + mix, BF16),
            pltpu.VMEM((chips,) + mix, BF16),
            pltpu.VMEM((chips,) + mix, BF16),
            pltpu.VMEM(mix, BF16),
            dma((12,)), dma((12,)),
            dma((sections, chips)), dma((sections, chips)), dma((chips,)), dma((chips,)),
            dma((chips,)), dma((chips,)), dma((sections,)), dma((sections,)),
            dma((2, reps)), dma((2, reps)), dma((9,)), dma((9,)),
        ],
        compiler_params=pltpu.CompilerParams(
            collective_id=collective_id, has_side_effects=True, vmem_limit_bytes=VMEM_LIMIT
        ),
    )(x, c, w, g)


def chain_kernel(scale, x_ref, z_ref, m_ref, keep_ref, out_ref, scal_ref):
    sections = keep_ref.shape[1]
    head = scal_ref.shape[1]
    rows, width = keep_ref.shape[0], x_ref.shape[1]
    wide = 4 * head
    start = pl.multiple_of(lax.axis_index("section") * rows, rows)
    x_float = x_ref[pl.ds(start, rows), :].astype(F32)
    square = jnp.sum(x_float * x_float, axis=1, keepdims=True)
    z = [jnp.sum(z_ref[s].astype(F32), axis=0) for s in range(sections)]
    base = sections // 2 * 3 * head
    mix = [
        jnp.concatenate([m_ref[c, s].reshape(head // 2, -1) for c in range(2)], axis=0)
        for s in range(sections)
    ]

    def pair(low, high):
        gap = high - low
        owner = low
        if gap > sections // 2:
            owner, gap = high, sections - gap
        return mix[owner][:, (gap - 1) * 3 * head : gap * 3 * head]

    row = lax.broadcasted_iota(jnp.int32, (rows, rows), 0)
    col = lax.broadcasted_iota(jnp.int32, (rows, rows), 1)
    allowed = (row >= col) & (row // ROWS == col // ROWS)
    y = [z[s][:, 0 : 3 * head] for s in range(sections)]
    acto = [z[s][:, 3 * head : wide] for s in range(sections)]
    saved = []
    for s in range(sections):
        keep = keep_ref[:, s : s + 1]
        rinv = lax.rsqrt(jnp.maximum(square, 0.0) / width + EPSILON)
        qkv = (y[s] * rinv).astype(BF16)
        query, key, value = qkv[:, 0:head], qkv[:, head : 2 * head], qkv[:, 2 * head :]
        scores = dot(query, key, ((1,), (1,))) * scale
        expo = jnp.exp(jnp.where(allowed, scores, -1e30))
        probs = expo / jnp.sum(expo, axis=1, keepdims=True)
        low = probs.astype(BF16)
        heads = dot(low, value).astype(BF16)
        kept = heads.astype(F32) * keep
        kept_low = kept.astype(BF16)
        saved.append((rinv, query, key, value, probs, low, acto[:], y[s]))
        out_ref[0, :, s * head : (s + 1) * head] = heads
        moved = dot(kept_low, mix[s][:, base:])
        square = square + jnp.sum(
            kept * (2.0 * acto[s] + moved[:, s * head : (s + 1) * head]),
            axis=1,
            keepdims=True,
        )
        for t in range(sections):
            if t > s:
                y[t] = y[t] + dot(kept_low, pair(s, t))
            acto[t] = acto[t] + moved[:, t * head : (t + 1) * head]
    bo = [z[s][:, wide:] for s in range(sections)]
    lane = lax.broadcasted_iota(jnp.int32, (rows, head), 1)
    scal = jnp.zeros((rows, head), F32)
    for s in range(sections - 1, -1, -1):
        keep = keep_ref[:, s : s + 1]
        rinv, query, key, value, probs, low, act_o, y_s = saved[s]
        d_heads = (keep * bo[s]).astype(BF16)
        d_value = dot(low, d_heads, ((0,), (0,))).astype(BF16)
        d_probs = dot(d_heads, value, ((1,), (1,)))
        d_score = (
            probs * (d_probs - jnp.sum(probs * d_probs, axis=1, keepdims=True)) * scale
        ).astype(BF16)
        d_query = dot(d_score, key).astype(BF16)
        d_key = dot(d_score, query, ((0,), (0,))).astype(BF16)
        grads = jnp.concatenate([d_query, d_key, d_value], axis=1)
        out_ref[1, :, s * head : (s + 1) * head] = d_value
        out_ref[2, :, s * head : (s + 1) * head] = d_query
        out_ref[3, :, s * head : (s + 1) * head] = d_key
        mean = jnp.sum(grads.astype(F32) * y_s, axis=1, keepdims=True) / width
        pull = rinv * rinv * rinv * mean
        scal = jnp.where(lane == s, rinv, scal)
        scal = jnp.where(lane == sections + s, pull, scal)
        for t in range(s):
            part = dot(grads, pair(t, s), ((1,), (1,)))
            bo[t] = bo[t] + rinv * part - pull * act_o[t]
    scal_ref[...] = scal


def tail_kernel(
    x_ref, c_ref, made_ref, scal_ref, keep_ref, w_ref, g_ref,
    out_ref,
    made, scal, normed, acts, part, relay, from_x, from_y, merged,
    z_send, z_recv, core_send, core_recv, h_send, h_recv,
):
    reps, rows, shard = x_ref.shape
    sections = w_ref.shape[0]
    head = w_ref.shape[2] // 4
    qkv = 3 * head
    half = shard // 2
    chips = reps // 2
    total = reps * rows
    core, chip, section, partner, along, _ = place(chips, 1)
    other = 1 - core
    near_x = section + 1 - 2 * lax.rem(section, 2)
    near_y = lax.rem(section + 2, 4)
    diagonal = 3 - section
    to_x, to_y = {"section": near_x}, {"section": near_y}
    greet([partner] + [a[3] for a in along] + [to_x, to_y])
    outs = [made.at[i] for i in range(4)] + [scal]
    ins = [made_ref.at[i] for i in range(4)] + [scal_ref]
    sends = []

    def start(copy):
        copy.start()
        sends.append(copy)

    for i in (4, 0, 1, 2, 3):
        for step, to, source, target in along:
            at = outs[i].at[core, chip]
            start(remote(ins[i], at, z_send.at[i, step], z_recv.at[i, step], target))
        at = outs[i].at[core, chip]
        start(remote(ins[i], at, core_send.at[i, 0], core_recv.at[i, 0], partner))
    for i in range(4):
        made[i, core, chip] = made_ref[i]
    scal[core, chip] = scal_ref[...]

    def arrive(kinds):
        for i in kinds:
            for step, to, source, target in along:
                at = outs[i].at[core, source]
                remote(at, at, z_send.at[i, step], z_recv.at[i, step], target).wait_recv()
                start(remote(at, at, core_send.at[i, step], core_recv.at[i, step], partner))
        for i in kinds:
            for step, source in [(0, chip)] + [(a[0], a[2]) for a in along]:
                at = outs[i].at[other, source]
                remote(at, at, core_send.at[i, step], core_recv.at[i, step], partner).wait_recv()

    first, second = pl.ds(0, half), pl.ds(half, half)

    def message(kind, number, src, dst, target):
        return remote(src, dst, h_send.at[kind, number], h_recv.at[kind, number], target)

    def messages(kind):
        p = part.at[kind]
        return [
            message(kind, 0, p.at[diagonal, first], relay.at[kind, 0], to_x),
            message(kind, 1, p.at[near_x, first], from_x.at[kind, first], to_x),
            message(kind, 2, merged.at[kind, 1], from_x.at[kind, second], to_x),
            message(kind, 3, p.at[diagonal, second], relay.at[kind, 1], to_y),
            message(kind, 4, p.at[near_y, second], from_y.at[kind, second], to_y),
            message(kind, 5, merged.at[kind, 0], from_y.at[kind, first], to_y),
        ]

    def send_parts(kind):
        copies = messages(kind)
        for number in (0, 3, 1, 4):
            start(copies[number])

    def send_merged(kind):
        copies = messages(kind)
        copies[0].wait_recv()
        merged[kind, 0] = (
            relay[kind, 0].astype(F32) + part[kind, near_y, 0:half].astype(F32)
        ).astype(BF16)
        start(copies[5])
        copies[3].wait_recv()
        merged[kind, 1] = (
            relay[kind, 1].astype(F32) + part[kind, near_x, half:].astype(F32)
        ).astype(BF16)
        start(copies[2])

    def block(kind, s):
        return made[kind, :, :, :, s * head : (s + 1) * head].reshape(total, head)

    def column(at):
        return scal[:, :, :, at : at + 1].reshape(total, 1)

    over = ((0,), (0,))
    across = ((1,), (1,))
    arrive((4, 0, 1))
    act = x_ref[...].reshape(total, shard).astype(F32)
    for s in range(sections):
        acts[s] = act.astype(BF16)
        normed[s] = (act * column(s) * g_ref[s]).astype(BF16)
        part[2, s] = dot(normed[s], block(1, s), over).astype(BF16)
        if s + 1 < sections:
            push = dot(block(0, s), w_ref[s, :, qkv:], across)
            act = (act + keep_ref[:, s : s + 1] * push).astype(BF16).astype(F32)
    send_parts(2)
    arrive((2,))
    for s in range(sections):
        part[0, s] = dot(normed[s], block(2, s), over).astype(BF16)
    send_parts(0)
    arrive((3,))
    for s in range(sections):
        part[1, s] = dot(normed[s], block(3, s), over).astype(BF16)
    send_merged(2)
    send_parts(1)
    back = c_ref[...].reshape(total, shard).astype(F32)
    for s in range(sections - 1, -1, -1):
        grad_rows = (keep_ref[:, s : s + 1] * back).astype(BF16)
        part[3, s] = dot(grad_rows, block(0, s), over).astype(BF16)
        if s > 0:
            d_normed = dot(block(2, s), w_ref[s, :, 0:head], across)
            d_normed = d_normed + dot(block(3, s), w_ref[s, :, head : 2 * head], across)
            d_normed = d_normed + dot(block(1, s), w_ref[s, :, 2 * head : qkv], across)
            pull = column(sections + s)
            back = back + column(s) * (d_normed * g_ref[s]) - pull * acts[s].astype(F32)
            back = back.astype(BF16).astype(F32)
    send_merged(0)
    send_parts(3)
    send_merged(1)

    def finish(kind):
        copies = messages(kind)
        for number in (1, 2, 4, 5):
            copies[number].wait_recv()
        out_ref[kind] = (
            part[kind, section].astype(F32)
            + from_x[kind].astype(F32)
            + from_y[kind].astype(F32)
        )

    finish(2)
    send_merged(3)
    finish(0)
    finish(1)
    finish(3)
    for copy in sends:
        copy.wait_send()


def tail_call(x, c, made, scal, keep, w, g, collective_id):
    reps, rows, shard = x.shape
    sections = w.shape[0]
    head = w.shape[2] // 4
    total, half = reps * rows, shard // 2
    chips = reps // 2
    dma = pltpu.SemaphoreType.DMA
    return pl.pallas_call(
        tail_kernel,
        out_shape=[jax.ShapeDtypeStruct((4, shard, head), F32)],
        in_specs=vmem_specs(7),
        out_specs=vmem_specs(1),
        scratch_shapes=[
            pltpu.VMEM((4, 2, chips) + made.shape[1:], BF16),
            pltpu.VMEM((2, chips) + scal.shape, F32),
            pltpu.VMEM((sections, total, shard), BF16),
            pltpu.VMEM((sections, total, shard), BF16),
            pltpu.VMEM((4, sections, shard, head), BF16),
            pltpu.VMEM((4, 2, half, head), BF16),
            pltpu.VMEM((4, shard, head), BF16),
            pltpu.VMEM((4, shard, head), BF16),
            pltpu.VMEM((4, 2, half, head), BF16),
            dma((5, chips)), dma((5, chips)), dma((5, chips)), dma((5, chips)),
            dma((4, 6)), dma((4, 6)),
        ],
        compiler_params=pltpu.CompilerParams(
            collective_id=collective_id, has_side_effects=True, vmem_limit_bytes=VMEM_LIMIT
        ),
    )(x, c, made, scal, keep, w, g)


def local_call(kernel, shapes, *arrays):
    return pl.pallas_call(
        kernel,
        out_shape=shapes,
        in_specs=vmem_specs(len(arrays)),
        out_specs=vmem_specs(len(shapes)),
        compiler_params=pltpu.CompilerParams(vmem_limit_bytes=VMEM_LIMIT),
    )(*arrays)


def low_rank(x_in, cot, w_q, w_k, w_v, w_out, gains, offsets, counts):
    sections = lax.axis_size("section")
    reps = lax.axis_size("rep")
    section_pos = lax.axis_index("section")
    rep_pos = lax.axis_index("rep")
    width = x_in.shape[1]
    shard, head = w_q.shape[1:]
    batches = MB // sections
    chips = reps // 2
    rows = batches * ROWS
    wide = 4 * head
    w_pack = jnp.concatenate([w_q[0], w_k[0], w_v[0], w_out[0]], axis=1)
    g_own = lax.dynamic_slice_in_dim(gains, rep_pos * shard, shard, 1)
    running = jnp.zeros_like(offsets[0])
    landed = []
    for s in range(sections):
        running = running + offsets[s]
        landed.append(running % reps)
    landed = jnp.stack(landed)
    my_batches = lax.dynamic_slice_in_dim(landed, section_pos * batches, batches, 1)
    rep_ids = jnp.arange(reps, dtype=jnp.int32)
    slots = (rep_ids % chips) * 2 + rep_ids // chips
    landing = (slots[None, :, None] + my_batches[:, None, :]) % reps
    match = landing[..., None] == rep_ids
    allowed = jnp.sum(jnp.where(match, counts[:, None, None, :], 0), axis=-1)
    batch_ids = section_pos * batches + jnp.arange(batches, dtype=jnp.int32)
    keep = (batch_ids < allowed).astype(F32)
    keep = jnp.transpose(keep, (1, 2, 0))
    keep = jnp.broadcast_to(keep[:, :, None, :], (reps, batches, ROWS, sections))
    keep = keep.reshape(reps * rows, sections)
    keep_own = lax.dynamic_slice_in_dim(keep, slot("rep", rep_pos, reps) * rows, rows, 0)
    x_shard, c_shard, w_all, g_all, z, mixed = front_call(x_in, cot, w_pack, g_own, rows, 0)
    made, scal = local_call(
        functools.partial(chain_kernel, head ** (-0.5)),
        [
            jax.ShapeDtypeStruct((4, rows, sections * head), BF16),
            jax.ShapeDtypeStruct((rows, head), F32),
        ],
        x_in,
        z,
        mixed,
        keep_own,
    )
    (grads,) = tail_call(x_shard, c_shard, made, scal, keep, w_all, g_all, 2)
    return tuple(grads[i][None] for i in range(4))


def on_device(*arrays):
    sections = lax.axis_size("section")
    head = arrays[2].shape[2]
    reps = lax.axis_size("rep")
    if sections == 4 and reps == 8 and head % (16 * reps) == 0:
        return low_rank(*arrays)
    return pipelined(*arrays)


def solution(mesh):
    in_specs = (
        P("rep", None),
        P("rep", None),
        P("section", "rep", None),
        P("section", "rep", None),
        P("section", "rep", None),
        P("section", "rep", None),
        P("section", None),
        P(),
        P(),
    )
    out_specs = (
        P("section", "rep", None),
        P("section", "rep", None),
        P("section", "rep", None),
        P("section", "rep", None),
    )
    return jax.shard_map(
        on_device, mesh=mesh, in_specs=in_specs, out_specs=out_specs, check_vma=False
    )
```
